32 devices in a mesh: gx: 4 (over z), gz: 2 (over x), gy: 4 (over y, core).
Axes of the slice: x: 2, y: 2, z: 4, core: 2. Of those that a mesh axis runs over, the one named last changes fastest.
Arguments:
- velocity: float32 [3, 512, 512, 512], P(None, ('gx', 'gz'), None, 'gy'), may hold values from -5 to 5, as said below
- spacing: float32 [513], replicated, may hold values from 0.15 to 3.4, as said below
Outputs:
- pressure: float32 [512, 512, 512], P(('gx', 'gz'), None, 'gy')
The draws below stay inside these ranges and needn't reach their ends.
Inputs may be any that keep to these rules, and one draw needn't show every extreme that they name: `velocity`: velocity components at the grid nodes. `spacing`: entry 0 is the gap from the lower wall to the first node and entry 512 the gap from the last node to the upper wall.
All inputs are finite; a program needn't handle non-finite values.
Results may differ from the reference program's by a relative error of at most 0.0003.
Values sent between devices are 32-bit elements; how exact they have to be, the bound alone decides.
A program may use at most 256 MiB of HBM per device.

```python
import math
import jax
import jax.numpy as jnp
from jax import lax

NX = 512
NY = 512
NZ = 512


def draw_velocity(key, part):
    values = jnp.clip(jax.random.normal(key, (3, NZ, NX, NY), jnp.float32), -5.0, 5.0)
    return values


def draw_spacing(key, part):
    index = jnp.arange(NY + 1, dtype=jnp.float32)
    profile = 1.0 - 0.7 * jnp.cos(2.0 * math.pi * (index + 0.5) / (NY + 1))
    factor = jnp.exp(jax.random.uniform(key, (NY + 1,), jnp.float32, math.log(0.6), math.log(1.5)))
    return profile * factor


def setup_inputs(seed: int = 0) -> dict:
    splits = jax.random.split(jax.random.key(seed), 3)
    velocity = draw_velocity(jax.random.fold_in(splits[2], 71), 0)
    spacing = draw_spacing(jax.random.fold_in(splits[2], 71), 0)
    return dict(velocity=velocity, spacing=spacing)


span_step = 0.5


def wave_numbers(length, step_size):
    index = jnp.arange(length)
    wave = jnp.where(index == 1, length // 2, index // 2)
    return (2.0 * math.pi / (length * step_size)) * wave.astype(jnp.float32)


def to_modes(field, axis):
    moved = jnp.moveaxis(field, axis, -1)
    length = moved.shape[-1]
    half = length // 2
    spectrum = jnp.fft.rfft(moved, axis=-1)
    real_part = jnp.real(spectrum)[..., :half]
    imag_part = jnp.concatenate([jnp.real(spectrum)[..., half:half + 1], jnp.imag(spectrum)[..., 1:half]], axis=-1)
    packed = jnp.stack([real_part, imag_part], axis=-1).reshape(moved.shape)
    return jnp.moveaxis(packed, -1, axis)


def from_modes(packed, axis):
    moved = jnp.moveaxis(packed, axis, -1)
    length = moved.shape[-1]
    real_part = moved[..., 0::2]
    imag_part = moved[..., 1::2]
    zeros = jnp.zeros_like(real_part[..., :1])
    spectrum_real = jnp.concatenate([real_part, imag_part[..., :1]], axis=-1)
    spectrum_imag = jnp.concatenate([zeros, imag_part[..., 1:], zeros], axis=-1)
    values = jnp.fft.irfft(spectrum_real + 1j * spectrum_imag, n=length, axis=-1)
    return jnp.moveaxis(values, -1, axis)


def derivative(packed, axis, step_size):
    moved = jnp.moveaxis(packed, axis, -1)
    length = moved.shape[-1]
    half = length // 2
    kappa = (2.0 * math.pi / (length * step_size)) * jnp.arange(half).astype(jnp.float32)
    real_part = moved[..., 0::2]
    imag_part = moved[..., 1::2]
    result = jnp.stack([-kappa * imag_part, kappa * real_part], axis=-1).reshape(moved.shape)
    return jnp.moveaxis(result, -1, axis)


def reference(velocity, spacing):
    width = spacing[:-1] + spacing[1:]
    lower = 2.0 / (width * spacing[:-1])
    upper = 2.0 / (width * spacing[1:])
    padded = jnp.pad(velocity[1], ((0, 0), (0, 0), (1, 1)))
    normal_slope = (padded[..., 2:] - padded[..., :-2]) / width
    flow_part = derivative(to_modes(velocity[0], 1), 1, 1.0) + to_modes(normal_slope, 1)
    span_part = to_modes(velocity[2], 1)
    source = to_modes(flow_part, 0) + derivative(to_modes(span_part, 0), 0, span_step)
    sigma = wave_numbers(NZ, span_step)[:, None] ** 2 + wave_numbers(NX, 1.0)[None, :] ** 2
    diagonal = -(lower + upper)
    lower_row = lower.at[0].set(0.0)
    upper_row = upper.at[-1].set(0.0)

    def solve_block(pair):
        block, sigma_block = pair
        start = jnp.zeros(sigma_block.shape, jnp.float32)

        def forward(carry, row):
            ratio, value = carry
            side, lower_value, diagonal_value, upper_value = row
            pivot = diagonal_value - sigma_block - lower_value * ratio
            ratio_next = upper_value / pivot
            value_next = (side - lower_value * value) / pivot
            return (ratio_next, value_next), (ratio_next, value_next)

        rows_first = jnp.moveaxis(block, -1, 0)
        unused, (ratios, values) = lax.scan(forward, (start, start), (rows_first, lower_row, diagonal, upper_row))

        def backward(after, row):
            ratio, value = row
            current = value - ratio * after
            return current, current

        unused, solved = lax.scan(backward, start, (ratios, values), reverse=True)
        return jnp.moveaxis(solved, 0, -1)

    blocks = 8
    modes = lax.map(solve_block, (source.reshape(blocks, NZ // blocks, NX, NY), sigma.reshape(blocks, NZ // blocks, NX)))
    modes = modes.reshape(NZ, NX, NY)
    return from_modes(from_modes(modes, 0), 1)
```

```python
import functools
import math

import jax
import jax.numpy as jnp
from jax import lax
from jax.experimental import pallas as pl
from jax.experimental.pallas import tpu as pltpu
from jax.sharding import PartitionSpec as P

span_step = 0.5
f32 = jnp.float32
bf16 = jnp.bfloat16
MESH = pl.DeviceIdType.MESH


def halos(field):
    size = lax.axis_size("gy")
    up = [(i, i + 1) for i in range(size - 1)]
    down = [(j, i) for i, j in up]
    before = lax.ppermute(field[:, :, -1], "gy", up)
    after = lax.ppermute(field[:, :, 0], "gy", down)
    return before, after


def wave_of(mode, length):
    return jnp.where(mode == 1, length // 2, lax.shift_right_logical(mode, 1))


def wave_cosine(phase, length):
    if length & (length - 1):
        phase = lax.rem(phase, length)
    else:
        phase = jnp.bitwise_and(phase, length - 1)
    phase = jnp.where(phase >= length // 2, phase - length, phase)
    return jnp.cos(2.0 * math.pi / length * phase.astype(f32))


def is_sine(mode):
    return jnp.logical_and(jnp.bitwise_and(mode, 1) == 1, mode >= 3)


def forward_entry(mode, point, length):
    phase = point * wave_of(mode, length)
    return wave_cosine(phase + jnp.where(is_sine(mode), length // 4, 0), length)


def derive_entry(mode, point, length, step_size):
    wave = wave_of(mode, length)
    phase = point * wave + jnp.where(is_sine(mode), 0, 3 * length // 4)
    kappa = 2.0 * math.pi / (length * step_size) * wave.astype(f32)
    return wave_cosine(phase, length) * jnp.where(mode >= 2, kappa, 0.0)


def inverse_entry(mode, point, length):
    weight = jnp.where(mode >= 2, 2.0, 1.0) / length
    return forward_entry(mode, point, length) * weight


def square_entry(mode, length, step_size):
    kappa = 2.0 * math.pi / (length * step_size) * wave_of(mode, length).astype(f32)
    return kappa * kappa


def halves(value):
    top = value.astype(bf16)
    return top, (value - top.astype(f32)).astype(bf16)


def product(left, right, turned=False):
    dims = (((1,), (1 if turned else 0,)), ((), ()))

    def one(a, b):
        return lax.dot_general(a, b, dims, preferred_element_type=f32)

    return one(left[0], right[0]) + (one(left[0], right[1]) + one(left[1], right[0]))


def solve(side_ref, ratio_ref, lower_ref, upper_ref, sigma, count, total):
    half = total // 2
    zero = jnp.zeros_like(sigma)

    def rows(row):
        return pl.ds(row, count, stride=total)

    def eliminate(step, carry):
        ratio, value, ratio_up, value_up = carry
        low, high_row = step, total - 1 - step
        lower, upper = lower_ref[low], upper_ref[low]
        inverse = 1.0 / (-(lower + upper) - sigma - lower * ratio)
        ratio = upper * inverse
        value = (side_ref[rows(low), :] - lower * value) * inverse
        ratio_ref[low] = ratio
        side_ref[rows(low), :] = value
        lower, upper = lower_ref[high_row], upper_ref[high_row]
        inverse = 1.0 / (-(lower + upper) - sigma - upper * ratio_up)
        ratio_up = lower * inverse
        value_up = (side_ref[rows(high_row), :] - upper * value_up) * inverse
        ratio_ref[high_row] = ratio_up
        side_ref[rows(high_row), :] = value_up
        return ratio, value, ratio_up, value_up

    ratio, value, ratio_up, value_up = lax.fori_loop(
        0, half, eliminate, (zero, zero, zero, zero), unroll=4
    )
    down = (value - ratio * value_up) / (1.0 - ratio * ratio_up)
    up = value_up - ratio_up * down
    side_ref[rows(half - 1), :] = down
    side_ref[rows(half), :] = up

    def substitute(step, carry):
        down, up = carry
        low, high_row = half - 2 - step, half + 1 + step
        down = side_ref[rows(low), :] - ratio_ref[low] * down
        up = side_ref[rows(high_row), :] - ratio_ref[high_row] * up
        side_ref[rows(low), :] = down
        side_ref[rows(high_row), :] = up
        return down, up

    lax.fori_loop(0, half - 1, substitute, (down, up))


def kernel(
    sizes, step, lower_ref, upper_ref, gap_ref, before_ref, after_ref, velocity, result, staged,
    landed, returned, back_staged, flow_top, flow_low, slope_top, slope_low, span_top,
    span_low, curl_top, curl_low, inverse_top, inverse_low, loaded, columns, ratio, outgoing,
    modes_in, planes_out, send_flow, recv_flow, send_y, recv_y, send_home, recv_home, send_back,
    recv_back, load_sem, local_sem,
):
    size_x, size_z, size_y, planes, length, rows, parts, count = sizes
    group = size_x * size_z
    span = planes * group
    mode_count = parts * count
    share = span // size_y
    total = rows * size_y
    here_x, here_z, here_y = (lax.axis_index(a) for a in ("gx", "gz", "gy"))
    own = here_x * size_z + here_z

    def target(shift):
        far_x = lax.rem(here_x + shift // size_z, size_x)
        far_z = lax.rem(here_z + lax.rem(shift, size_z), size_z)
        return far_x, far_z, far_x * size_z + far_z

    def origin(shift):
        far_x = lax.rem(here_x + size_x - shift // size_z, size_x)
        far_z = lax.rem(here_z + size_z - lax.rem(shift, size_z), size_z)
        return far_x * size_z + far_z

    def each(first, last, act):
        def turn(index, carry):
            act(index)
            return carry

        lax.fori_loop(first, last, turn, 0)

    def put(top_ref, low_ref, at, value):
        top, low = halves(value)
        top_ref[at] = top
        low_ref[at] = low

    def iota(shape, axis):
        return lax.broadcasted_iota(jnp.int32, shape, axis)

    def flow_tables(index):
        part, owner = index // group, lax.rem(index, group)
        mode = owner * mode_count + part * count + iota((count, length), 0)
        point = iota((count, length), 1)
        at = pl.ds(pl.multiple_of(index * count, count), count)
        put(flow_top, flow_low, at, forward_entry(mode, point, length))
        put(slope_top, slope_low, at, derive_entry(mode, point, length, 1.0))

    def span_tables(index):
        at = pl.ds(pl.multiple_of(index * 16, 16), 16)
        line = index * 16 + iota((16, span), 0)
        across = iota((16, span), 1)
        put(span_top, span_low, at, forward_entry(line, across, span))
        put(curl_top, curl_low, at, derive_entry(line, across, span, span_step))
        put(inverse_top, inverse_low, at, inverse_entry(across, line, span))

    def emit(part, kind):
        block = group * count
        at = pl.ds(pl.multiple_of(part * block, block), block)
        out_spec = pl.BlockSpec((group, step, count, rows), lambda i: (0, i, 0, 0))
        in_spec = pl.BlockSpec((step, length, rows), lambda i: (i, 0, 0))

        def write(out, pair, value):
            for n in range(2):
                half = value[:, n * rows : (n + 1) * rows]
                out[:, pair + n] = half.reshape(group, count, rows)

        def span_body(indices, w, out):
            for pair in range(0, step, 2):
                field = jnp.concatenate([w[pair], w[pair + 1]], axis=1)
                write(out, pair, product((flow_top[at], flow_low[at]), halves(field)))

        def slope_of(v, plane):
            lane = iota((length, rows), 1)
            ahead = pltpu.roll(v, rows - 1, 1)
            behind = pltpu.roll(v, 1, 1)
            low = pltpu.roll(before_ref[...], lax.rem(rows - plane, rows), 1)
            high = pltpu.roll(after_ref[...], rows - 1 - plane, 1)
            ahead = jnp.where(lane == rows - 1, high, ahead)
            behind = jnp.where(lane == 0, low, behind)
            return (ahead - behind) * gap_ref[0:1, :]

        def flow_body(indices, u, v, out):
            first = indices.index[0] * step
            for pair in range(0, step, 2):
                field = jnp.concatenate([u[pair], u[pair + 1]], axis=1)
                value = product((slope_top[at], slope_low[at]), halves(field))
                field = jnp.concatenate(
                    [slope_of(v[pair + n], first + pair + n) for n in range(2)], axis=1
                )
                value = value + product((flow_top[at], flow_low[at]), halves(field))
                write(out, pair, value)

        if kind == 0:
            pltpu.emit_pipeline(
                span_body, grid=(planes // step,), in_specs=[in_spec], out_specs=[out_spec],
                _explicit_indices=True,
            )(velocity.at[2], staged.at[part, 0])
        else:
            pltpu.emit_pipeline(
                flow_body, grid=(planes // step,), in_specs=[in_spec] * 2, out_specs=[out_spec],
                _explicit_indices=True,
            )(velocity.at[0], velocity.at[1], staged.at[part, 1])

    def flow_copy(part, kind, shift):
        far_x, far_z, far = target(shift)
        return pltpu.make_async_remote_copy(
            staged.at[part, kind, far],
            landed.at[part, kind, own],
            send_flow.at[part, kind, shift],
            recv_flow.at[part, kind, shift],
            device_id=(far_x, far_z, here_y),
            device_id_type=MESH,
        )

    def y_copy(part, shift):
        far = lax.rem(here_y + shift, size_y)
        return pltpu.make_async_remote_copy(
            outgoing.at[far],
            columns.at[part, :, pl.ds(pl.multiple_of(here_y * rows, rows), rows), :],
            send_y.at[part, shift],
            recv_y.at[part, shift],
            device_id=(here_x, here_z, far),
            device_id_type=MESH,
        )

    def home_copy(part, shift):
        far = lax.rem(here_y + shift, size_y)
        return pltpu.make_async_remote_copy(
            columns.at[part, :, pl.ds(pl.multiple_of(far * rows, rows), rows), :],
            returned.at[part, here_y],
            send_home.at[part, shift],
            recv_home.at[part, shift],
            device_id=(here_x, here_z, far),
            device_id_type=MESH,
        )

    def back_copy(part, shift):
        far_x, far_z, far = target(shift)
        return pltpu.make_async_remote_copy(
            back_staged.at[part, :, pl.ds(pl.multiple_of(far * planes, planes), planes), :],
            result.at[pl.ds(own * mode_count + part * count, count)],
            send_back.at[part, shift],
            recv_back.at[part, shift],
            device_id=(far_x, far_z, here_y),
            device_id_type=MESH,
        )

    each(0, parts * group, flow_tables)

    def forward(part):
        for kind in range(2):
            emit(part, kind)
            each(1, group, lambda shift: flow_copy(part, kind, shift).start())

    each(0, parts, forward)
    each(0, span // 16, span_tables)

    def middle(part):
        def load(kind, shift):
            owner = origin(shift)
            at = pl.ds(pl.multiple_of(owner * planes * count, planes * count), planes * count)
            return pltpu.make_async_copy(
                landed.at[part, kind, owner].reshape(planes * count, rows),
                loaded.at[kind, at],
                load_sem.at[kind, shift],
            )

        def load_own(kind):
            at = pl.ds(pl.multiple_of(own * planes * count, planes * count), planes * count)
            return pltpu.make_async_copy(
                staged.at[part, kind, own].reshape(planes * count, rows),
                loaded.at[kind, at],
                load_sem.at[kind, 0],
            )

        for kind in range(2):
            load_own(kind).start()

        def fetch(shift):
            for kind in range(2):
                flow_copy(part, kind, shift).wait_recv()
                load(kind, shift).start()

        each(1, group, fetch)
        for kind in range(2):
            load_own(kind).wait()

        def fetched(shift):
            for kind in range(2):
                load(kind, shift).wait()

        each(1, group, fetched)

        def transform(pair):
            value = None
            for kind, table in ((0, (curl_top, curl_low)), (1, (span_top, span_low))):
                field = jnp.concatenate(
                    [loaded[kind, pl.ds(pair * 2 + n, span, stride=count), :] for n in range(2)],
                    axis=1,
                )
                term = product((table[0][...], table[1][...]), halves(field))
                value = term if value is None else value + term
            for n in range(2):
                turned = value[:, n * rows : (n + 1) * rows].T
                for far in range(size_y):
                    outgoing[far, pair * 2 + n] = turned[:, far * share : (far + 1) * share]

        each(0, count // 2, transform)
        keep = pltpu.make_async_copy(
            outgoing.at[here_y],
            columns.at[part, :, pl.ds(pl.multiple_of(here_y * rows, rows), rows), :],
            local_sem.at[0],
        )
        keep.start()
        each(1, size_y, lambda shift: y_copy(part, shift).start())
        keep.wait()
        each(1, size_y, lambda shift: y_copy(part, shift).wait())
        mode = own * mode_count + part * count + iota((count, share), 0)
        span_mode = here_y * share + iota((count, share), 1)
        sigma = square_entry(mode, length, 1.0) + square_entry(span_mode, span, span_step)
        solve(
            columns.at[part].reshape(count * total, share), ratio, lower_ref, upper_ref, sigma,
            count, total,
        )
        keep = pltpu.make_async_copy(
            columns.at[part, :, pl.ds(pl.multiple_of(here_y * rows, rows), rows), :],
            modes_in.at[here_y],
            local_sem.at[0],
        )
        keep.start()
        each(1, size_y, lambda shift: home_copy(part, shift).start())

        def come(shift):
            home_copy(part, shift).wait()
            far = lax.rem(here_y + size_y - shift, size_y)
            copy = pltpu.make_async_copy(
                returned.at[part, far], modes_in.at[far], load_sem.at[0, shift]
            )
            copy.start()
            copy.wait()

        each(1, size_y, come)
        keep.wait()

        def restore(pair):
            field = jnp.concatenate(
                [
                    jnp.concatenate([modes_in[k, pair * 2 + n] for k in range(size_y)], axis=1)
                    for n in range(2)
                ],
                axis=0,
            )
            value = product((inverse_top[...], inverse_low[...]), halves(field), True)
            for n in range(2):
                planes_out[pair * 2 + n] = value[:, n * rows : (n + 1) * rows]

        each(0, count // 2, restore)
        stage = pltpu.make_async_copy(planes_out, back_staged.at[part], local_sem.at[0])
        keep = pltpu.make_async_copy(
            planes_out.at[:, pl.ds(pl.multiple_of(own * planes, planes), planes), :],
            result.at[pl.ds(own * mode_count + part * count, count)],
            local_sem.at[1],
        )
        stage.start()
        keep.start()
        stage.wait()
        each(1, group, lambda shift: back_copy(part, shift).start())
        keep.wait()

    each(0, parts, middle)

    def drain(part):
        def one(shift):
            back_copy(part, shift).wait()
            for kind in range(2):
                flow_copy(part, kind, shift).wait_send()

        each(1, group, one)

    each(0, parts, drain)


def local(velocity, spacing):
    planes, length, rows = velocity.shape[1:]
    size_x, size_z, size_y = (lax.axis_size(a) for a in ("gx", "gz", "gy"))
    group = size_x * size_z
    span = planes * group
    mode_count = length // group
    parts = 4
    while parts > 1 and (mode_count % parts or (mode_count // parts) % 8):
        parts //= 2
    count = mode_count // parts
    share = span // size_y
    total = rows * size_y
    step = 4
    gaps = lax.dynamic_slice_in_dim(spacing, lax.axis_index("gy") * rows, rows + 1)
    gap = jnp.broadcast_to(1.0 / (gaps[:-1] + gaps[1:]), (8, rows))
    full_width = spacing[:-1] + spacing[1:]
    lower = 2.0 / (full_width * spacing[:-1])
    upper = 2.0 / (full_width * spacing[1:])
    before, after = (
        jnp.pad(side.T, ((0, 0), (0, rows - planes))) for side in halos(velocity[1])
    )
    vmem = pl.BlockSpec(memory_space=pltpu.VMEM)
    smem = pl.BlockSpec(memory_space=pltpu.SMEM)
    hbm = pl.BlockSpec(memory_space=pltpu.HBM)
    dma = pltpu.SemaphoreType.DMA
    outs = pl.pallas_call(
        functools.partial(
            kernel, (size_x, size_z, size_y, planes, length, rows, parts, count), step
        ),
        out_shape=[
            jax.ShapeDtypeStruct((length, planes, rows), f32),
            jax.ShapeDtypeStruct((parts, 2, group, planes, count, rows), f32),
            jax.ShapeDtypeStruct((parts, 2, group, planes, count, rows), f32),
            jax.ShapeDtypeStruct((parts, size_y, count, rows, share), f32),
            jax.ShapeDtypeStruct((parts, count, span, rows), f32),
        ],
        in_specs=[smem, smem, vmem, vmem, vmem, hbm],
        out_specs=[hbm] * 5,
        scratch_shapes=[pltpu.VMEM((length, length), bf16)] * 4
        + [pltpu.VMEM((span, span), bf16)] * 6
        + [
            pltpu.VMEM((2, span * count, rows), f32),
            pltpu.VMEM((parts, count, total, share), f32),
            pltpu.VMEM((total, count, share), f32),
            pltpu.VMEM((size_y, count, rows, share), f32),
            pltpu.VMEM((size_y, count, rows, share), f32),
            pltpu.VMEM((count, span, rows), f32),
            dma((parts, 2, group)),
            dma((parts, 2, group)),
            dma((parts, size_y)),
            dma((parts, size_y)),
            dma((parts, size_y)),
            dma((parts, size_y)),
            dma((parts, group)),
            dma((parts, group)),
            dma((2, max(group, size_y))),
            dma((2,)),
        ],
        compiler_params=pltpu.CompilerParams(
            has_side_effects=True, vmem_limit_bytes=67043328
        ),
    )(lower, upper, gap, before, after, velocity)
    modes = jnp.arange(length, dtype=jnp.int32)
    inverse = inverse_entry(modes[None, :], modes[:, None], length)
    return jnp.einsum(
        "mzy,xm->zxy", outs[0], inverse, precision=lax.Precision.HIGH, preferred_element_type=f32
    )


def solution(mesh):
    return jax.shard_map(
        local,
        mesh=mesh,
        in_specs=(P(None, ("gx", "gz"), None, "gy"), P()),
        out_specs=P(("gx", "gz"), None, "gy"),
        check_vma=False,
    )
```

```python
import functools
import math

import jax
import jax.numpy as jnp
from jax import lax
from jax.experimental import pallas as pl
from jax.experimental.pallas import tpu as pltpu
from jax.sharding import PartitionSpec as P

span_step = 0.5
f32 = jnp.float32
bf16 = jnp.bfloat16
MESH = pl.DeviceIdType.MESH


def split_by(value, size):
    if size & (size - 1):
        return lax.div(value, size), lax.rem(value, size)
    return lax.shift_right_logical(value, size.bit_length() - 1), jnp.bitwise_and(value, size - 1)


def wave_of(mode, length):
    return jnp.where(mode == 1, length // 2, lax.shift_right_logical(mode, 1))


def wave_cosine(phase, length):
    if length & (length - 1):
        phase = lax.rem(phase, length)
    else:
        phase = jnp.bitwise_and(phase, length - 1)
    phase = jnp.where(phase >= length // 2, phase - length, phase)
    return jnp.cos(2.0 * math.pi / length * phase.astype(f32))


def is_sine(mode):
    return jnp.logical_and(jnp.bitwise_and(mode, 1) == 1, mode >= 3)


def forward_entry(mode, point, length):
    phase = point * wave_of(mode, length)
    return wave_cosine(phase + jnp.where(is_sine(mode), length // 4, 0), length)


def derive_entry(mode, point, length, step_size):
    wave = wave_of(mode, length)
    phase = point * wave + jnp.where(is_sine(mode), 0, 3 * length // 4)
    kappa = 2.0 * math.pi / (length * step_size) * wave.astype(f32)
    return wave_cosine(phase, length) * jnp.where(mode >= 2, kappa, 0.0)


def inverse_entry(mode, point, length):
    weight = jnp.where(mode >= 2, 2.0, 1.0) / length
    return forward_entry(mode, point, length) * weight


def square_entry(mode, length, step_size):
    kappa = 2.0 * math.pi / (length * step_size) * wave_of(mode, length).astype(f32)
    return kappa * kappa


def halves(value):
    top = value.astype(bf16)
    return top, (value - top.astype(f32)).astype(bf16)


def product(left, right, turned=False):
    dims = (((1,), (1 if turned else 0,)), ((), ()))

    def one(a, b):
        return lax.dot_general(a, b, dims, preferred_element_type=f32)

    return one(left[0], right[0]) + (one(left[0], right[1]) + one(left[1], right[0]))


def solve(side_ref, ratio_ref, sides_ref, sigma, count, total):
    half = total // 2
    zero = jnp.zeros_like(sigma)

    def rows(row):
        return pl.ds(row, count, stride=total)

    def eliminate(step, carry):
        ratio, value, ratio_up, value_up = carry
        low, high_row = step, total - 1 - step
        lower, upper = sides_ref[0, low], sides_ref[1, low]
        inverse = 1.0 / (-(lower + upper) - sigma - lower * ratio)
        ratio = upper * inverse
        value = (side_ref[rows(low), :] - lower * value) * inverse
        ratio_ref[low] = ratio
        side_ref[rows(low), :] = value
        lower, upper = sides_ref[0, high_row], sides_ref[1, high_row]
        inverse = 1.0 / (-(lower + upper) - sigma - upper * ratio_up)
        ratio_up = lower * inverse
        value_up = (side_ref[rows(high_row), :] - upper * value_up) * inverse
        ratio_ref[high_row] = ratio_up
        side_ref[rows(high_row), :] = value_up
        return ratio, value, ratio_up, value_up

    ratio, value, ratio_up, value_up = lax.fori_loop(
        0, half, eliminate, (zero, zero, zero, zero), unroll=4
    )
    down = (value - ratio * value_up) / (1.0 - ratio * ratio_up)
    up = value_up - ratio_up * down
    side_ref[rows(half - 1), :] = down
    side_ref[rows(half), :] = up

    def substitute(step, carry):
        down, up = carry
        low, high_row = half - 2 - step, half + 1 + step
        down = side_ref[rows(low), :] - ratio_ref[low] * down
        up = side_ref[rows(high_row), :] - ratio_ref[high_row] * up
        side_ref[rows(low), :] = down
        side_ref[rows(high_row), :] = up
        return down, up

    lax.fori_loop(0, half - 1, substitute, (down, up))


def kernel(
    sizes, step, sides_ref, gap_ref, velocity, result, summed, table_top, table_low, staged,
    landed, returned, back_staged, flow_top, flow_low, slope_top, slope_low, span_top,
    span_low, curl_top, curl_low, inverse_top, inverse_low, last_top, last_low, edges, before_ref,
    after_ref, loaded, columns, ratio, outgoing, modes_in, planes_out, send_edge, recv_edge,
    send_flow, recv_flow, send_y, recv_y, send_home, recv_home, send_back, recv_back, load_sem,
    local_sem,
):
    size_x, size_z, size_y, planes, length, rows, parts, count = sizes
    group = size_x * size_z
    span = planes * group
    mode_count = parts * count
    share = span // size_y
    total = rows * size_y
    here_x, here_z, here_y = (lax.axis_index(a) for a in ("gx", "gz", "gy"))
    own = here_x * size_z + here_z

    def target(shift):
        far_x = lax.rem(here_x + shift // size_z, size_x)
        far_z = lax.rem(here_z + lax.rem(shift, size_z), size_z)
        return far_x, far_z, far_x * size_z + far_z

    def origin(shift):
        far_x = lax.rem(here_x + size_x - shift // size_z, size_x)
        far_z = lax.rem(here_z + size_z - lax.rem(shift, size_z), size_z)
        return far_x * size_z + far_z

    def each(first, last, act):
        def turn(index, carry):
            act(index)
            return carry

        lax.fori_loop(first, last, turn, 0)

    def put(top_ref, low_ref, at, value):
        top, low = halves(value)
        top_ref[at] = top
        low_ref[at] = low

    def iota(shape, axis):
        return lax.broadcasted_iota(jnp.int32, shape, axis)

    def mode_at(slot):
        part, slot = split_by(slot, group * count)
        owner, slot = split_by(slot, count)
        return owner * mode_count + part * count + slot

    def flow_tables(index):
        at = pl.ds(pl.multiple_of(index * 16, 16), 16)
        mode = mode_at(index * 16 + iota((16, length), 0))
        point = iota((16, length), 1)
        put(flow_top, flow_low, at, forward_entry(mode, point, length))
        put(slope_top, slope_low, at, derive_entry(mode, point, length, 1.0))

    def last_tables(index):
        at = pl.ds(pl.multiple_of(index * 16, 16), 16)
        point = index * 16 + iota((16, length), 0)
        mode = mode_at(iota((16, length), 1))
        put(last_top, last_low, at, inverse_entry(mode, point, length))

    def span_tables(index):
        at = pl.ds(pl.multiple_of(index * 16, 16), 16)
        line = index * 16 + iota((16, span), 0)
        across = iota((16, span), 1)
        put(span_top, span_low, at, forward_entry(line, across, span))
        put(curl_top, curl_low, at, derive_entry(line, across, span, span_step))
        put(inverse_top, inverse_low, at, inverse_entry(across, line, span))

    def emit(part, kind):
        block = group * count
        at = pl.ds(pl.multiple_of(part * block, block), block)
        out_spec = pl.BlockSpec((group, step, count, rows), lambda i: (0, i, 0, 0))
        in_spec = pl.BlockSpec((step, length, rows), lambda i: (i, 0, 0))

        def write(out, pair, value):
            for n in range(2):
                half = value[:, n * rows : (n + 1) * rows]
                out[:, pair + n] = half.reshape(group, count, rows)

        def span_body(indices, w, out):
            for pair in range(0, step, 2):
                field = jnp.concatenate([w[pair], w[pair + 1]], axis=1)
                write(out, pair, product((flow_top[at], flow_low[at]), halves(field)))

        def slope_of(v, plane):
            lane = iota((length, rows), 1)
            ahead = pltpu.roll(v, rows - 1, 1)
            behind = pltpu.roll(v, 1, 1)
            low = pltpu.roll(before_ref[...], lax.rem(rows - plane, rows), 1)
            high = pltpu.roll(after_ref[...], rows - 1 - plane, 1)
            ahead = jnp.where(lane == rows - 1, high, ahead)
            behind = jnp.where(lane == 0, low, behind)
            return (ahead - behind) * gap_ref[here_y, 0:1, :]

        def flow_body(indices, u, v, out):
            first = indices.index[0] * step
            for pair in range(0, step, 2):
                field = jnp.concatenate([u[pair], u[pair + 1]], axis=1)
                value = product((slope_top[at], slope_low[at]), halves(field))
                field = jnp.concatenate(
                    [slope_of(v[pair + n], first + pair + n) for n in range(2)], axis=1
                )
                value = value + product((flow_top[at], flow_low[at]), halves(field))
                write(out, pair, value)

        if kind == 0:
            pltpu.emit_pipeline(
                span_body, grid=(planes // step,), in_specs=[in_spec], out_specs=[out_spec],
                _explicit_indices=True,
            )(velocity.at[2], staged.at[part, 0])
        else:
            pltpu.emit_pipeline(
                flow_body, grid=(planes // step,), in_specs=[in_spec] * 2, out_specs=[out_spec],
                _explicit_indices=True,
            )(velocity.at[0], velocity.at[1], staged.at[part, 1])

    def edge_body(indices, v):
        lane = iota((length, rows), 1)
        for n in range(step):
            plane = indices.index[0] * step + n
            here = lane == plane
            edges[0] = jnp.where(here, pltpu.roll(v[n], plane, 1), edges[0])
            edges[1] = jnp.where(here, pltpu.roll(v[n], lax.rem(plane + 1, rows), 1), edges[1])

    def edge_copy(side):
        far = lax.rem(here_y + (size_y - 1, 1)[side], size_y)
        return pltpu.make_async_remote_copy(
            edges.at[side],
            (after_ref, before_ref)[side],
            send_edge.at[side],
            recv_edge.at[side],
            device_id=(here_x, here_z, far),
            device_id_type=MESH,
        )

    def flow_copy(part, kind, shift):
        far_x, far_z, far = target(shift)
        return pltpu.make_async_remote_copy(
            staged.at[part, kind, far],
            landed.at[part, kind, own],
            send_flow.at[part, kind, shift],
            recv_flow.at[part, kind, shift],
            device_id=(far_x, far_z, here_y),
            device_id_type=MESH,
        )

    def y_copy(part, shift):
        far = lax.rem(here_y + shift, size_y)
        return pltpu.make_async_remote_copy(
            outgoing.at[far],
            columns.at[part, :, pl.ds(pl.multiple_of(here_y * rows, rows), rows), :],
            send_y.at[part, shift],
            recv_y.at[part, shift],
            device_id=(here_x, here_z, far),
            device_id_type=MESH,
        )

    def home_copy(part, shift):
        far = lax.rem(here_y + shift, size_y)
        return pltpu.make_async_remote_copy(
            columns.at[part, :, pl.ds(pl.multiple_of(far * rows, rows), rows), :],
            returned.at[part, here_y],
            send_home.at[part, shift],
            recv_home.at[part, shift],
            device_id=(here_x, here_z, far),
            device_id_type=MESH,
        )

    def back_copy(part, shift):
        far_x, far_z, far = target(shift)
        return pltpu.make_async_remote_copy(
            back_staged.at[part, :, pl.ds(pl.multiple_of(far * planes, planes), planes), :],
            result.at[part, own],
            send_back.at[part, shift],
            recv_back.at[part, shift],
            device_id=(far_x, far_z, here_y),
            device_id_type=MESH,
        )

    first = group * count // 16
    each(0, first, flow_tables)

    def forward(part, kind):
        emit(part, kind)
        each(1, group, lambda shift: flow_copy(part, kind, shift).start())

    forward(0, 0)
    edges[...] = jnp.zeros_like(edges)
    pltpu.emit_pipeline(
        edge_body,
        grid=(planes // step,),
        in_specs=[pl.BlockSpec((step, length, rows), lambda i: (i, 0, 0))],
        _explicit_indices=True,
    )(velocity.at[1])
    for side in range(2):
        edge_copy(side).start()
    each(first, length // 16, flow_tables)
    for side in range(2):
        edge_copy(side).wait()
    before_ref[...] = jnp.where(here_y == 0, 0.0, before_ref[...])
    after_ref[...] = jnp.where(here_y == size_y - 1, 0.0, after_ref[...])
    forward(0, 1)

    def forward_both(part):
        forward(part, 0)
        forward(part, 1)

    each(1, parts, forward_both)
    each(0, span // 16, span_tables)
    each(0, length // 16, last_tables)

    def middle(part):
        def load(kind, shift):
            owner = origin(shift)
            at = pl.ds(pl.multiple_of(owner * planes * count, planes * count), planes * count)
            return pltpu.make_async_copy(
                landed.at[part, kind, owner].reshape(planes * count, rows),
                loaded.at[kind, at],
                load_sem.at[kind, shift],
            )

        def load_own(kind):
            at = pl.ds(pl.multiple_of(own * planes * count, planes * count), planes * count)
            return pltpu.make_async_copy(
                staged.at[part, kind, own].reshape(planes * count, rows),
                loaded.at[kind, at],
                load_sem.at[kind, 0],
            )

        for kind in range(2):
            load_own(kind).start()

        def fetch(shift):
            for kind in range(2):
                flow_copy(part, kind, shift).wait_recv()
                load(kind, shift).start()

        each(1, group, fetch)
        for kind in range(2):
            load_own(kind).wait()

        def fetched(shift):
            for kind in range(2):
                load(kind, shift).wait()

        each(1, group, fetched)

        def transform(pair):
            value = None
            for kind, table in ((0, (curl_top, curl_low)), (1, (span_top, span_low))):
                field = jnp.concatenate(
                    [loaded[kind, pl.ds(pair * 2 + n, span, stride=count), :] for n in range(2)],
                    axis=1,
                )
                term = product((table[0][...], table[1][...]), halves(field))
                value = term if value is None else value + term
            for n in range(2):
                turned = value[:, n * rows : (n + 1) * rows].T
                for far in range(size_y):
                    outgoing[far, pair * 2 + n] = turned[:, far * share : (far + 1) * share]

        each(0, count // 2, transform)
        keep = pltpu.make_async_copy(
            outgoing.at[here_y],
            columns.at[part, :, pl.ds(pl.multiple_of(here_y * rows, rows), rows), :],
            local_sem.at[0],
        )
        keep.start()
        each(1, size_y, lambda shift: y_copy(part, shift).start())
        keep.wait()
        each(1, size_y, lambda shift: y_copy(part, shift).wait())
        mode = own * mode_count + part * count + iota((count, share), 0)
        span_mode = here_y * share + iota((count, share), 1)
        sigma = square_entry(mode, length, 1.0) + square_entry(span_mode, span, span_step)
        solve(
            columns.at[part].reshape(count * total, share), ratio, sides_ref, sigma, count, total
        )
        keep = pltpu.make_async_copy(
            columns.at[part, :, pl.ds(pl.multiple_of(here_y * rows, rows), rows), :],
            modes_in.at[here_y],
            local_sem.at[0],
        )
        keep.start()
        each(1, size_y, lambda shift: home_copy(part, shift).start())

        def come(shift):
            home_copy(part, shift).wait()
            far = lax.rem(here_y + size_y - shift, size_y)
            copy = pltpu.make_async_copy(
                returned.at[part, far], modes_in.at[far], load_sem.at[0, shift]
            )
            copy.start()
            copy.wait()

        each(1, size_y, come)
        keep.wait()

        def restore(pair):
            field = jnp.concatenate(
                [
                    jnp.concatenate([modes_in[k, pair * 2 + n] for k in range(size_y)], axis=1)
                    for n in range(2)
                ],
                axis=0,
            )
            value = product((inverse_top[...], inverse_low[...]), halves(field), True)
            for n in range(2):
                planes_out[pair * 2 + n] = value[:, n * rows : (n + 1) * rows]

        each(0, count // 2, restore)
        stage = pltpu.make_async_copy(planes_out, back_staged.at[part], local_sem.at[0])
        keep = pltpu.make_async_copy(
            planes_out.at[:, pl.ds(pl.multiple_of(own * planes, planes), planes), :],
            result.at[part, own],
            local_sem.at[1],
        )
        stage.start()
        keep.start()
        stage.wait()
        each(1, group, lambda shift: back_copy(part, shift).start())
        keep.wait()

    each(0, parts, middle)
    tables = [
        pltpu.make_async_copy(source, target_ref, local_sem.at[n])
        for n, (source, target_ref) in enumerate(((last_top, table_top), (last_low, table_low)))
    ]
    for copy in tables:
        copy.start()
    for copy in tables:
        copy.wait()

    def arrive(part):
        each(1, group, lambda shift: back_copy(part, shift).wait_recv())

    each(0, parts - 1, arrive)
    if parts > 1:
        depth = (parts - 1) * group * count

        def sum_body(indices, r, out):
            gather(r, last_top[:, :depth], last_low[:, :depth], None, out)

        pltpu.emit_pipeline(
            sum_body,
            grid=(planes // 8,),
            in_specs=[pl.BlockSpec((depth, 8, rows), lambda i: (0, i, 0))],
            out_specs=[pl.BlockSpec((8, length, rows), lambda i: (i, 0, 0))],
            _explicit_indices=True,
        )(result.at[pl.ds(0, parts - 1)].reshape(depth, planes, rows), summed)
    arrive(parts - 1)

    def drain(part):
        def one(shift):
            back_copy(part, shift).wait_send()
            for kind in range(2):
                flow_copy(part, kind, shift).wait_send()

        each(1, group, one)

    each(0, parts, drain)


def gather(r, top, low, base, out):
    depth, step, rows = r.shape
    flat = r.reshape(depth * step, rows)
    for pair in range(0, step, 2):
        field = jnp.concatenate(
            [flat[pl.ds(pair + n, depth, stride=step), :] for n in range(2)], axis=1
        )
        value = product((top, low), halves(field))
        for n in range(2):
            half = value[:, n * rows : (n + 1) * rows]
            out[pair + n] = half if base is None else half + base[pair + n]


def finish_kernel(depth, r, top, low, *refs):
    base = refs[0] if len(refs) > 1 else None
    width = top.shape[1]
    gather(r, top[:, width - depth :], low[:, width - depth :], base, refs[-1])


def finish(result, summed, top, low, parts):
    length, rows = top.shape[0], result.shape[-1]
    planes = result.shape[-2]
    depth = length // parts
    plane_spec = pl.BlockSpec((8, length, rows), lambda i: (i, 0, 0))
    table_spec = pl.BlockSpec((length, length), lambda i: (0, 0))
    bases = [summed] if parts > 1 else []
    cells = planes * length * rows
    return pl.pallas_call(
        functools.partial(finish_kernel, depth),
        grid=(planes // 8,),
        out_shape=jax.ShapeDtypeStruct((planes, length, rows), f32),
        in_specs=[
            pl.BlockSpec((depth, 8, rows), lambda i: (parts - 1, i, 0)),
            table_spec,
            table_spec,
        ]
        + [plane_spec] * len(bases),
        out_specs=plane_spec,
        compiler_params=pltpu.CompilerParams(vmem_limit_bytes=40 << 20),
        cost_estimate=pl.CostEstimate(
            flops=6 * cells * depth, bytes_accessed=8 * cells, transcendentals=0
        ),
    )(result.reshape(length, planes, rows), top, low, *bases)


def local(velocity, spacing):
    planes, length, rows = velocity.shape[1:]
    size_x, size_z, size_y = (lax.axis_size(a) for a in ("gx", "gz", "gy"))
    group = size_x * size_z
    span = planes * group
    mode_count = length // group
    parts = max(mode_count // 8, 1)
    count = mode_count // parts
    share = span // size_y
    total = rows * size_y
    step = 4
    full_width = spacing[:-1] + spacing[1:]
    sides = jnp.stack([2.0 / (full_width * spacing[:-1]), 2.0 / (full_width * spacing[1:])])
    gap = jnp.broadcast_to((1.0 / full_width).reshape(size_y, 1, rows), (size_y, 8, rows))
    vmem = pl.BlockSpec(memory_space=pltpu.VMEM)
    smem = pl.BlockSpec(memory_space=pltpu.SMEM)
    hbm = pl.BlockSpec(memory_space=pltpu.HBM)
    dma = pltpu.SemaphoreType.DMA
    outs = pl.pallas_call(
        functools.partial(
            kernel, (size_x, size_z, size_y, planes, length, rows, parts, count), step
        ),
        out_shape=[
            jax.ShapeDtypeStruct((parts, group, count, planes, rows), f32),
            jax.ShapeDtypeStruct((planes, length, rows) if parts > 1 else (8, rows), f32),
            jax.ShapeDtypeStruct((length, length), bf16),
            jax.ShapeDtypeStruct((length, length), bf16),
            jax.ShapeDtypeStruct((parts, 2, group, planes, count, rows), f32),
            jax.ShapeDtypeStruct((parts, 2, group, planes, count, rows), f32),
            jax.ShapeDtypeStruct((parts, size_y, count, rows, share), f32),
            jax.ShapeDtypeStruct((parts, count, span, rows), f32),
        ],
        in_specs=[smem, vmem, hbm],
        out_specs=[hbm] * 8,
        scratch_shapes=[pltpu.VMEM((length, length), bf16)] * 4
        + [pltpu.VMEM((span, span), bf16)] * 6
        + [pltpu.VMEM((length, length), bf16)] * 2
        + [
            pltpu.VMEM((2, length, rows), f32),
            pltpu.VMEM((length, rows), f32),
            pltpu.VMEM((length, rows), f32),
            pltpu.VMEM((2, span * count, rows), f32),
            pltpu.VMEM((parts, count, total, share), f32),
            pltpu.VMEM((total, count, share), f32),
            pltpu.VMEM((size_y, count, rows, share), f32),
            pltpu.VMEM((size_y, count, rows, share), f32),
            pltpu.VMEM((count, span, rows), f32),
            dma((2,)),
            dma((2,)),
            dma((parts, 2, group)),
            dma((parts, 2, group)),
            dma((parts, size_y)),
            dma((parts, size_y)),
            dma((parts, size_y)),
            dma((parts, size_y)),
            dma((parts, group)),
            dma((parts, group)),
            dma((2, max(group, size_y))),
            dma((2,)),
        ],
        compiler_params=pltpu.CompilerParams(
            has_side_effects=True, vmem_limit_bytes=67043328
        ),
    )(sides, gap, velocity)
    return finish(*outs[:4], parts)


def solution(mesh):
    return jax.shard_map(
        local,
        mesh=mesh,
        in_specs=(P(None, ("gx", "gz"), None, "gy"), P()),
        out_specs=P(("gx", "gz"), None, "gy"),
        check_vma=False,
    )
```

```python
import functools
import math

import jax
import jax.numpy as jnp
from jax import lax
from jax.experimental import pallas as pl
from jax.experimental.pallas import tpu as pltpu
from jax.sharding import PartitionSpec as P

span_step = 0.5
f32 = jnp.float32
bf16 = jnp.bfloat16
MESH = pl.DeviceIdType.MESH


def split_by(value, size):
    if size & (size - 1):
        return lax.div(value, size), lax.rem(value, size)
    return lax.shift_right_logical(value, size.bit_length() - 1), jnp.bitwise_and(value, size - 1)


def wave_of(mode, length):
    return jnp.where(mode == 1, length // 2, lax.shift_right_logical(mode, 1))


def wave_cosine(phase, length):
    if length & (length - 1):
        phase = lax.rem(phase, length)
    else:
        phase = jnp.bitwise_and(phase, length - 1)
    phase = jnp.where(phase >= length // 2, phase - length, phase)
    return jnp.cos(2.0 * math.pi / length * phase.astype(f32))


def is_sine(mode):
    return jnp.logical_and(jnp.bitwise_and(mode, 1) == 1, mode >= 3)


def forward_entry(mode, point, length):
    phase = point * wave_of(mode, length)
    return wave_cosine(phase + jnp.where(is_sine(mode), length // 4, 0), length)


def derive_entry(mode, point, length, step_size):
    wave = wave_of(mode, length)
    phase = point * wave + jnp.where(is_sine(mode), 0, 3 * length // 4)
    kappa = 2.0 * math.pi / (length * step_size) * wave.astype(f32)
    return wave_cosine(phase, length) * jnp.where(mode >= 2, kappa, 0.0)


def inverse_entry(mode, point, length):
    weight = jnp.where(mode >= 2, 2.0, 1.0) / length
    return forward_entry(mode, point, length) * weight


def square_entry(mode, length, step_size):
    kappa = 2.0 * math.pi / (length * step_size) * wave_of(mode, length).astype(f32)
    return kappa * kappa


def halves(value):
    top = value.astype(bf16)
    return top, (value - top.astype(f32)).astype(bf16)


def product(left, right, turned=False):
    dims = (((1,), (1 if turned else 0,)), ((), ()))

    def one(a, b):
        return lax.dot_general(a, b, dims, preferred_element_type=f32)

    return one(left[0], right[0]) + (one(left[0], right[1]) + one(left[1], right[0]))


def solve(side_ref, ratio_ref, sides_ref, sigma, count, total):
    half = total // 2
    zero = jnp.zeros_like(sigma)

    def rows(row):
        return pl.ds(row, count, stride=total)

    def eliminate(step, carry):
        ratio, value, ratio_up, value_up = carry
        low, high_row = step, total - 1 - step
        lower, upper = sides_ref[0, low], sides_ref[1, low]
        inverse = 1.0 / (-(lower + upper) - sigma - lower * ratio)
        ratio = upper * inverse
        value = (side_ref[rows(low), :] - lower * value) * inverse
        ratio_ref[low] = ratio
        side_ref[rows(low), :] = value
        lower, upper = sides_ref[0, high_row], sides_ref[1, high_row]
        inverse = 1.0 / (-(lower + upper) - sigma - upper * ratio_up)
        ratio_up = lower * inverse
        value_up = (side_ref[rows(high_row), :] - upper * value_up) * inverse
        ratio_ref[high_row] = ratio_up
        side_ref[rows(high_row), :] = value_up
        return ratio, value, ratio_up, value_up

    ratio, value, ratio_up, value_up = lax.fori_loop(
        0, half, eliminate, (zero, zero, zero, zero), unroll=4
    )
    down = (value - ratio * value_up) / (1.0 - ratio * ratio_up)
    up = value_up - ratio_up * down
    side_ref[rows(half - 1), :] = down
    side_ref[rows(half), :] = up

    def substitute(step, carry):
        down, up = carry
        low, high_row = half - 2 - step, half + 1 + step
        down = side_ref[rows(low), :] - ratio_ref[low] * down
        up = side_ref[rows(high_row), :] - ratio_ref[high_row] * up
        side_ref[rows(low), :] = down
        side_ref[rows(high_row), :] = up
        return down, up

    lax.fori_loop(0, half - 1, substitute, (down, up))


def kernel(
    sizes, step, sides_ref, gap_ref, velocity, result, summed, tail_table, staged,
    landed, returned, back_staged, flow_top, flow_low, slope_top, slope_low, span_top,
    span_low, curl_top, curl_low, inverse_top, inverse_low, last_top, last_low, tail, edges, before_ref,
    after_ref, loaded, columns, ratio, outgoing, modes_in, planes_out, send_edge, recv_edge,
    send_flow, recv_flow, send_y, recv_y, send_home, recv_home, send_back, recv_back, load_sem,
    local_sem,
):
    size_x, size_z, size_y, planes, length, rows, parts, count = sizes
    group = size_x * size_z
    span = planes * group
    mode_count = parts * count
    share = span // size_y
    total = rows * size_y
    here_x, here_z, here_y = (lax.axis_index(a) for a in ("gx", "gz", "gy"))
    own = here_x * size_z + here_z

    def target(shift):
        far_x = lax.rem(here_x + shift // size_z, size_x)
        far_z = lax.rem(here_z + lax.rem(shift, size_z), size_z)
        return far_x, far_z, far_x * size_z + far_z

    def origin(shift):
        far_x = lax.rem(here_x + size_x - shift // size_z, size_x)
        far_z = lax.rem(here_z + size_z - lax.rem(shift, size_z), size_z)
        return far_x * size_z + far_z

    def each(first, last, act):
        def turn(index, carry):
            act(index)
            return carry

        lax.fori_loop(first, last, turn, 0)

    def each_far(act):
        def turn(index):
            place, side = index // size_z, lax.rem(index, size_z)
            far = jnp.where(here_x < size_x // 2, size_x - 1 - place, place)
            shift = lax.rem(far - here_x + size_x, size_x) * size_z + side

            @pl.when(shift > 0)
            def _():
                act(shift)

        each(0, group, turn)

    def put(top_ref, low_ref, at, value):
        top, low = halves(value)
        top_ref[at] = top
        low_ref[at] = low

    def iota(shape, axis):
        return lax.broadcasted_iota(jnp.int32, shape, axis)

    def mode_at(slot):
        part, slot = split_by(slot, group * count)
        owner, slot = split_by(slot, count)
        return owner * mode_count + part * count + slot

    def flow_tables(index):
        at = pl.ds(pl.multiple_of(index * 16, 16), 16)
        mode = mode_at(index * 16 + iota((16, length), 0))
        point = iota((16, length), 1)
        put(flow_top, flow_low, at, forward_entry(mode, point, length))
        put(slope_top, slope_low, at, derive_entry(mode, point, length, 1.0))

    def last_tables(index):
        at = pl.ds(pl.multiple_of(index * 16, 16), 16)
        point = index * 16 + iota((16, length), 0)
        mode = mode_at(iota((16, length), 1))
        put(last_top, last_low, at, inverse_entry(mode, point, length))

    def span_tables(index):
        at = pl.ds(pl.multiple_of(index * 16, 16), 16)
        line = index * 16 + iota((16, span), 0)
        across = iota((16, span), 1)
        put(span_top, span_low, at, forward_entry(line, across, span))
        put(curl_top, curl_low, at, derive_entry(line, across, span, span_step))
        put(inverse_top, inverse_low, at, inverse_entry(across, line, span))

    def emit(part, kind, start=0, size=planes):
        block = group * count
        at = pl.ds(pl.multiple_of(part * block, block), block)
        out_spec = pl.BlockSpec((group, step, count, rows), lambda i: (0, i, 0, 0))
        in_spec = pl.BlockSpec((step, length, rows), lambda i: (i, 0, 0))

        def write(out, pair, value):
            for n in range(2):
                half = value[:, n * rows : (n + 1) * rows]
                out[:, pair + n] = half.reshape(group, count, rows)

        def span_body(indices, w, out):
            for pair in range(0, step, 2):
                field = jnp.concatenate([w[pair], w[pair + 1]], axis=1)
                write(out, pair, product((flow_top[at], flow_low[at]), halves(field)))

        def slope_of(v, plane):
            lane = iota((length, rows), 1)
            ahead = pltpu.roll(v, rows - 1, 1)
            behind = pltpu.roll(v, 1, 1)
            low = pltpu.roll(before_ref[...], lax.rem(rows - plane, rows), 1)
            high = pltpu.roll(after_ref[...], rows - 1 - plane, 1)
            ahead = jnp.where(lane == rows - 1, high, ahead)
            behind = jnp.where(lane == 0, low, behind)
            return (ahead - behind) * gap_ref[here_y, 0:1, :]

        def flow_body(indices, u, v, out):
            first = indices.index[0] * step
            for pair in range(0, step, 2):
                field = jnp.concatenate([u[pair], u[pair + 1]], axis=1)
                value = product((slope_top[at], slope_low[at]), halves(field))
                field = jnp.concatenate(
                    [slope_of(v[pair + n], first + pair + n) for n in range(2)], axis=1
                )
                value = value + product((flow_top[at], flow_low[at]), halves(field))
                write(out, pair, value)

        if kind == 0:
            at_planes = pl.ds(start, size)
            pltpu.emit_pipeline(
                span_body, grid=(size // step,), in_specs=[in_spec], out_specs=[out_spec],
                _explicit_indices=True,
            )(velocity.at[2, at_planes], staged.at[part, 0, :, at_planes])
        else:
            pltpu.emit_pipeline(
                flow_body, grid=(planes // step,), in_specs=[in_spec] * 2, out_specs=[out_spec],
                _explicit_indices=True,
            )(velocity.at[0], velocity.at[1], staged.at[part, 1])

    def edge_body(indices, v):
        lane = iota((length, rows), 1)
        for n in range(step):
            plane = indices.index[0] * step + n
            here = lane == plane
            edges[0] = jnp.where(here, pltpu.roll(v[n], plane, 1), edges[0])
            edges[1] = jnp.where(here, pltpu.roll(v[n], lax.rem(plane + 1, rows), 1), edges[1])

    def edge_copy(side):
        far = lax.rem(here_y + (size_y - 1, 1)[side], size_y)
        return pltpu.make_async_remote_copy(
            edges.at[side],
            (after_ref, before_ref)[side],
            send_edge.at[side],
            recv_edge.at[side],
            device_id=(here_x, here_z, far),
            device_id_type=MESH,
        )

    def flow_copy(part, kind, shift, start=0, size=planes):
        far_x, far_z, far = target(shift)
        return pltpu.make_async_remote_copy(
            staged.at[part, kind, far, pl.ds(start, size)],
            landed.at[part, kind, own, pl.ds(start, size)],
            send_flow.at[part, kind, shift],
            recv_flow.at[part, kind, shift],
            device_id=(far_x, far_z, here_y),
            device_id_type=MESH,
        )

    def y_copy(part, shift):
        far = lax.rem(here_y + shift, size_y)
        return pltpu.make_async_remote_copy(
            outgoing.at[far],
            columns.at[part, :, pl.ds(pl.multiple_of(here_y * rows, rows), rows), :],
            send_y.at[part, shift],
            recv_y.at[part, shift],
            device_id=(here_x, here_z, far),
            device_id_type=MESH,
        )

    def home_copy(part, shift):
        far = lax.rem(here_y + shift, size_y)
        return pltpu.make_async_remote_copy(
            columns.at[part, :, pl.ds(pl.multiple_of(far * rows, rows), rows), :],
            returned.at[part, here_y],
            send_home.at[part, shift],
            recv_home.at[part, shift],
            device_id=(here_x, here_z, far),
            device_id_type=MESH,
        )

    def back_copy(part, shift):
        far_x, far_z, far = target(shift)
        return pltpu.make_async_remote_copy(
            back_staged.at[part, :, pl.ds(pl.multiple_of(far * planes, planes), planes), :],
            result.at[part, own],
            send_back.at[part, shift],
            recv_back.at[part, shift],
            device_id=(far_x, far_z, here_y),
            device_id_type=MESH,
        )

    first = group * count // 16
    each(0, first, flow_tables)

    def forward(part, kind):
        emit(part, kind)
        each_far(lambda shift: flow_copy(part, kind, shift).start())

    early = min(planes, 16)
    for start in range(0, planes, early):
        emit(0, 0, start, early)
        each_far(lambda shift: flow_copy(0, 0, shift, start, early).start())
    edges[...] = jnp.zeros_like(edges)
    pltpu.emit_pipeline(
        edge_body,
        grid=(planes // step,),
        in_specs=[pl.BlockSpec((step, length, rows), lambda i: (i, 0, 0))],
        _explicit_indices=True,
    )(velocity.at[1])
    for side in range(2):
        edge_copy(side).start()
    each(first, length // 16, flow_tables)
    for side in range(2):
        edge_copy(side).wait()
    before_ref[...] = jnp.where(here_y == 0, 0.0, before_ref[...])
    after_ref[...] = jnp.where(here_y == size_y - 1, 0.0, after_ref[...])
    forward(0, 1)

    def forward_both(part):
        forward(part, 0)
        forward(part, 1)

    each(1, parts, forward_both)
    each(0, span // 16, span_tables)
    each(0, length // 16, last_tables)

    def middle(part):
        def load(kind, shift):
            owner = origin(shift)
            at = pl.ds(pl.multiple_of(owner * planes * count, planes * count), planes * count)
            return pltpu.make_async_copy(
                landed.at[part, kind, owner].reshape(planes * count, rows),
                loaded.at[kind, at],
                load_sem.at[kind, shift],
            )

        def load_own(kind):
            at = pl.ds(pl.multiple_of(own * planes * count, planes * count), planes * count)
            return pltpu.make_async_copy(
                staged.at[part, kind, own].reshape(planes * count, rows),
                loaded.at[kind, at],
                load_sem.at[kind, 0],
            )

        for kind in range(2):
            load_own(kind).start()

        def fetch(shift):
            for kind in range(2):
                flow_copy(part, kind, shift).wait_recv()
                load(kind, shift).start()

        each(1, group, fetch)
        for kind in range(2):
            load_own(kind).wait()

        def fetched(shift):
            for kind in range(2):
                load(kind, shift).wait()

        each(1, group, fetched)

        def transform(pair):
            value = None
            for kind, table in ((0, (curl_top, curl_low)), (1, (span_top, span_low))):
                field = jnp.concatenate(
                    [loaded[kind, pl.ds(pair * 2 + n, span, stride=count), :] for n in range(2)],
                    axis=1,
                )
                term = product((table[0][...], table[1][...]), halves(field))
                value = term if value is None else value + term
            for n in range(2):
                turned = value[:, n * rows : (n + 1) * rows].T
                for far in range(size_y):
                    outgoing[far, pair * 2 + n] = turned[:, far * share : (far + 1) * share]

        each(0, count // 2, transform)
        keep = pltpu.make_async_copy(
            outgoing.at[here_y],
            columns.at[part, :, pl.ds(pl.multiple_of(here_y * rows, rows), rows), :],
            local_sem.at[0],
        )
        keep.start()
        each(1, size_y, lambda shift: y_copy(part, shift).start())
        keep.wait()
        each(1, size_y, lambda shift: y_copy(part, shift).wait())
        mode = own * mode_count + part * count + iota((count, share), 0)
        span_mode = here_y * share + iota((count, share), 1)
        sigma = square_entry(mode, length, 1.0) + square_entry(span_mode, span, span_step)
        solve(
            columns.at[part].reshape(count * total, share), ratio, sides_ref, sigma, count, total
        )
        keep = pltpu.make_async_copy(
            columns.at[part, :, pl.ds(pl.multiple_of(here_y * rows, rows), rows), :],
            modes_in.at[here_y],
            local_sem.at[0],
        )
        keep.start()
        each(1, size_y, lambda shift: home_copy(part, shift).start())

        def come(shift):
            home_copy(part, shift).wait()
            far = lax.rem(here_y + size_y - shift, size_y)
            copy = pltpu.make_async_copy(
                returned.at[part, far], modes_in.at[far], load_sem.at[0, shift]
            )
            copy.start()
            copy.wait()

        each(1, size_y, come)
        keep.wait()

        def restore(pair):
            field = jnp.concatenate(
                [
                    jnp.concatenate([modes_in[k, pair * 2 + n] for k in range(size_y)], axis=1)
                    for n in range(2)
                ],
                axis=0,
            )
            value = product((inverse_top[...], inverse_low[...]), halves(field), True)
            for n in range(2):
                planes_out[pair * 2 + n] = value[:, n * rows : (n + 1) * rows]

        each(0, count // 2, restore)
        stage = pltpu.make_async_copy(planes_out, back_staged.at[part], local_sem.at[0])
        keep = pltpu.make_async_copy(
            planes_out.at[:, pl.ds(pl.multiple_of(own * planes, planes), planes), :],
            result.at[part, own],
            local_sem.at[1],
        )
        stage.start()
        keep.start()
        stage.wait()
        each_far(lambda shift: back_copy(part, shift).start())
        keep.wait()

    each(0, parts, middle)
    depth = group * count
    tail[...] = jnp.concatenate(
        [table[:, length - depth :] for table in (last_top, last_top, last_low)], axis=1
    )
    copy = pltpu.make_async_copy(tail, tail_table, local_sem.at[0])
    copy.start()
    copy.wait()

    def arrive(part):
        each(1, group, lambda shift: back_copy(part, shift).wait_recv())

    each(0, parts - 1, arrive)
    if parts > 1:
        depth = (parts - 1) * group * count

        def sum_body(indices, r, out):
            gather(r, (last_top[:, :depth], last_low[:, :depth]), None, out)

        pltpu.emit_pipeline(
            sum_body,
            grid=(planes // 8,),
            in_specs=[pl.BlockSpec((depth, 8, rows), lambda i: (0, i, 0))],
            out_specs=[pl.BlockSpec((8, length, rows), lambda i: (i, 0, 0))],
            _explicit_indices=True,
        )(result.at[pl.ds(0, parts - 1)].reshape(depth, planes, rows), summed)
    arrive(parts - 1)

    def drain(part):
        def one(shift):
            back_copy(part, shift).wait_send()
            for kind in range(2):
                flow_copy(part, kind, shift).wait_send()

        each(1, group, one)

    each(0, parts, drain)


def gather(r, tables, base, out):
    depth, step, rows = r.shape
    flat = r.reshape(depth * step, rows)
    for pair in range(0, step, 2):
        field = jnp.concatenate(
            [flat[pl.ds(pair + n, depth, stride=step), :] for n in range(2)], axis=1
        )
        top, low = halves(field)
        if len(tables) == 1:
            stacked = jnp.concatenate([top, low, top], axis=0)
            value = jnp.dot(tables[0], stacked, preferred_element_type=f32)
        else:
            value = product(tables, (top, low))
        for n in range(2):
            half = value[:, n * rows : (n + 1) * rows]
            out[pair + n] = half if base is None else half + base[pair + n]


def finish_kernel(r, table, *refs):
    gather(r, (table[...],), refs[0] if len(refs) > 1 else None, refs[-1])


def finish(result, summed, table, parts):
    length, rows = table.shape[0], result.shape[-1]
    planes = result.shape[-2]
    depth = length // parts
    plane_spec = pl.BlockSpec((8, length, rows), lambda i: (i, 0, 0))
    bases = [summed] if parts > 1 else []
    cells = planes * length * rows
    return pl.pallas_call(
        finish_kernel,
        grid=(planes // 8,),
        out_shape=jax.ShapeDtypeStruct((planes, length, rows), f32),
        in_specs=[
            pl.BlockSpec((depth, 8, rows), lambda i: (parts - 1, i, 0)),
            pl.BlockSpec(table.shape, lambda i: (0, 0)),
        ]
        + [plane_spec] * len(bases),
        out_specs=plane_spec,
        compiler_params=pltpu.CompilerParams(vmem_limit_bytes=40 << 20),
        cost_estimate=pl.CostEstimate(
            flops=6 * cells * depth, bytes_accessed=8 * cells, transcendentals=0
        ),
    )(result.reshape(length, planes, rows), table, *bases)


def local(velocity, spacing):
    planes, length, rows = velocity.shape[1:]
    size_x, size_z, size_y = (lax.axis_size(a) for a in ("gx", "gz", "gy"))
    group = size_x * size_z
    span = planes * group
    mode_count = length // group
    parts = max(mode_count // 8, 1)
    count = mode_count // parts
    share = span // size_y
    total = rows * size_y
    step = 4
    full_width = spacing[:-1] + spacing[1:]
    sides = jnp.stack([2.0 / (full_width * spacing[:-1]), 2.0 / (full_width * spacing[1:])])
    gap = jnp.broadcast_to((1.0 / full_width).reshape(size_y, 1, rows), (size_y, 8, rows))
    vmem = pl.BlockSpec(memory_space=pltpu.VMEM)
    smem = pl.BlockSpec(memory_space=pltpu.SMEM)
    hbm = pl.BlockSpec(memory_space=pltpu.HBM)
    dma = pltpu.SemaphoreType.DMA
    outs = pl.pallas_call(
        functools.partial(
            kernel, (size_x, size_z, size_y, planes, length, rows, parts, count), step
        ),
        out_shape=[
            jax.ShapeDtypeStruct((parts, group, count, planes, rows), f32),
            jax.ShapeDtypeStruct((planes, length, rows) if parts > 1 else (8, rows), f32),
            jax.ShapeDtypeStruct((length, 3 * group * count), bf16),
            jax.ShapeDtypeStruct((parts, 2, group, planes, count, rows), f32),
            jax.ShapeDtypeStruct((parts, 2, group, planes, count, rows), f32),
            jax.ShapeDtypeStruct((parts, size_y, count, rows, share), f32),
            jax.ShapeDtypeStruct((parts, count, span, rows), f32),
        ],
        in_specs=[smem, vmem, hbm],
        out_specs=[hbm] * 7,
        scratch_shapes=[pltpu.VMEM((length, length), bf16)] * 4
        + [pltpu.VMEM((span, span), bf16)] * 6
        + [pltpu.VMEM((length, length), bf16)] * 2
        + [
            pltpu.VMEM((length, 3 * group * count), bf16),
            pltpu.VMEM((2, length, rows), f32),
            pltpu.VMEM((length, rows), f32),
            pltpu.VMEM((length, rows), f32),
            pltpu.VMEM((2, span * count, rows), f32),
            pltpu.VMEM((parts, count, total, share), f32),
            pltpu.VMEM((total, count, share), f32),
            pltpu.VMEM((size_y, count, rows, share), f32),
            pltpu.VMEM((size_y, count, rows, share), f32),
            pltpu.VMEM((count, span, rows), f32),
            dma((2,)),
            dma((2,)),
            dma((parts, 2, group)),
            dma((parts, 2, group)),
            dma((parts, size_y)),
            dma((parts, size_y)),
            dma((parts, size_y)),
            dma((parts, size_y)),
            dma((parts, group)),
            dma((parts, group)),
            dma((2, max(group, size_y))),
            dma((2,)),
        ],
        compiler_params=pltpu.CompilerParams(
            has_side_effects=True, vmem_limit_bytes=67043328
        ),
    )(sides, gap, velocity)
    return finish(*outs[:3], parts)


def solution(mesh):
    return jax.shard_map(
        local,
        mesh=mesh,
        in_specs=(P(None, ("gx", "gz"), None, "gy"), P()),
        out_specs=P(("gx", "gz"), None, "gy"),
        check_vma=False,
    )
```

```python
import functools
import math

import jax
import jax.numpy as jnp
from jax import lax
from jax.experimental import pallas as pl
from jax.experimental.pallas import tpu as pltpu
from jax.sharding import PartitionSpec as P

span_step = 0.5
f32 = jnp.float32
bf16 = jnp.bfloat16
MESH = pl.DeviceIdType.MESH


def split_by(value, size):
    if size & (size - 1):
        return lax.div(value, size), lax.rem(value, size)
    return lax.shift_right_logical(value, size.bit_length() - 1), jnp.bitwise_and(value, size - 1)


def wave_of(mode, length):
    return jnp.where(mode == 1, length // 2, lax.shift_right_logical(mode, 1))


def wave_cosine(phase, length):
    if length & (length - 1):
        phase = lax.rem(phase, length)
    else:
        phase = jnp.bitwise_and(phase, length - 1)
    phase = jnp.where(phase >= length // 2, phase - length, phase)
    return jnp.cos(2.0 * math.pi / length * phase.astype(f32))


def is_sine(mode):
    return jnp.logical_and(jnp.bitwise_and(mode, 1) == 1, mode >= 3)


def forward_entry(mode, point, length):
    phase = point * wave_of(mode, length)
    return wave_cosine(phase + jnp.where(is_sine(mode), length // 4, 0), length)


def derive_entry(mode, point, length, step_size):
    wave = wave_of(mode, length)
    phase = point * wave + jnp.where(is_sine(mode), 0, 3 * length // 4)
    kappa = 2.0 * math.pi / (length * step_size) * wave.astype(f32)
    return wave_cosine(phase, length) * jnp.where(mode >= 2, kappa, 0.0)


def inverse_entry(mode, point, length):
    weight = jnp.where(mode >= 2, 2.0, 1.0) / length
    return forward_entry(mode, point, length) * weight


def square_entry(mode, length, step_size):
    kappa = 2.0 * math.pi / (length * step_size) * wave_of(mode, length).astype(f32)
    return kappa * kappa


def halves(value):
    top = value.astype(bf16)
    return top, (value - top.astype(f32)).astype(bf16)


def product(left, right, turned=False):
    dims = (((1,), (1 if turned else 0,)), ((), ()))

    def one(a, b):
        return lax.dot_general(a, b, dims, preferred_element_type=f32)

    return one(left[0], right[0]) + (one(left[0], right[1]) + one(left[1], right[0]))


def solve(side_ref, ratio_ref, sides_ref, sigma, count, total):
    half = total // 2
    zero = jnp.zeros_like(sigma)

    def rows(row):
        return pl.ds(row, count, stride=total)

    def eliminate(step, carry):
        ratio, value, ratio_up, value_up = carry
        low, high_row = step, total - 1 - step
        lower, upper = sides_ref[0, low], sides_ref[1, low]
        inverse = 1.0 / (-(lower + upper) - sigma - lower * ratio)
        ratio = upper * inverse
        value = (side_ref[rows(low), :] - lower * value) * inverse
        ratio_ref[low] = ratio
        side_ref[rows(low), :] = value
        lower, upper = sides_ref[0, high_row], sides_ref[1, high_row]
        inverse = 1.0 / (-(lower + upper) - sigma - upper * ratio_up)
        ratio_up = lower * inverse
        value_up = (side_ref[rows(high_row), :] - upper * value_up) * inverse
        ratio_ref[high_row] = ratio_up
        side_ref[rows(high_row), :] = value_up
        return ratio, value, ratio_up, value_up

    ratio, value, ratio_up, value_up = lax.fori_loop(
        0, half, eliminate, (zero, zero, zero, zero), unroll=4
    )
    down = (value - ratio * value_up) / (1.0 - ratio * ratio_up)
    up = value_up - ratio_up * down
    side_ref[rows(half - 1), :] = down
    side_ref[rows(half), :] = up

    def substitute(step, carry):
        down, up = carry
        low, high_row = half - 2 - step, half + 1 + step
        down = side_ref[rows(low), :] - ratio_ref[low] * down
        up = side_ref[rows(high_row), :] - ratio_ref[high_row] * up
        side_ref[rows(low), :] = down
        side_ref[rows(high_row), :] = up
        return down, up

    lax.fori_loop(0, half - 1, substitute, (down, up))


def kernel(
    sizes, step, sides_ref, gap_ref, velocity, result, summed, tail_table, staged,
    landed, returned, back_staged, flow_top, flow_low, slope_top, slope_low, span_top,
    span_low, curl_top, curl_low, inverse_top, inverse_low, last_top, last_low, tail, edges, before_ref,
    after_ref, loaded, columns, ratio, outgoing, modes_in, planes_out, send_edge, recv_edge,
    send_flow, recv_flow, send_y, recv_y, send_home, recv_home, send_back, recv_back, load_sem,
    local_sem,
):
    size_x, size_z, size_y, planes, length, rows, parts, count = sizes
    group = size_x * size_z
    span = planes * group
    mode_count = parts * count
    share = span // size_y
    total = rows * size_y
    here_x, here_z, here_y = (lax.axis_index(a) for a in ("gx", "gz", "gy"))
    own = here_x * size_z + here_z

    def target(shift):
        far_x = lax.rem(here_x + shift // size_z, size_x)
        far_z = lax.rem(here_z + lax.rem(shift, size_z), size_z)
        return far_x, far_z, far_x * size_z + far_z

    def origin(shift):
        far_x = lax.rem(here_x + size_x - shift // size_z, size_x)
        far_z = lax.rem(here_z + size_z - lax.rem(shift, size_z), size_z)
        return far_x * size_z + far_z

    def each(first, last, act):
        def turn(index, carry):
            act(index)
            return carry

        lax.fori_loop(first, last, turn, 0)

    def put(top_ref, low_ref, at, value):
        top, low = halves(value)
        top_ref[at] = top
        low_ref[at] = low

    def iota(shape, axis):
        return lax.broadcasted_iota(jnp.int32, shape, axis)

    def mode_at(slot):
        part, slot = split_by(slot, group * count)
        owner, slot = split_by(slot, count)
        return owner * mode_count + part * count + slot

    def flow_tables(index):
        at = pl.ds(pl.multiple_of(index * 16, 16), 16)
        mode = mode_at(index * 16 + iota((16, length), 0))
        point = iota((16, length), 1)
        put(flow_top, flow_low, at, forward_entry(mode, point, length))
        put(slope_top, slope_low, at, derive_entry(mode, point, length, 1.0))

    def last_tables(index):
        at = pl.ds(pl.multiple_of(index * 16, 16), 16)
        point = index * 16 + iota((16, length), 0)
        mode = mode_at(iota((16, length), 1))
        put(last_top, last_low, at, inverse_entry(mode, point, length))

    def span_tables(index):
        at = pl.ds(pl.multiple_of(index * 16, 16), 16)
        line = index * 16 + iota((16, span), 0)
        across = iota((16, span), 1)
        put(span_top, span_low, at, forward_entry(line, across, span))
        put(curl_top, curl_low, at, derive_entry(line, across, span, span_step))
        put(inverse_top, inverse_low, at, inverse_entry(across, line, span))

    def emit(part, kind, start=0, size=planes):
        block = group * count
        at = pl.ds(pl.multiple_of(part * block, block), block)
        out_spec = pl.BlockSpec((group, step, count, rows), lambda i: (0, i, 0, 0))
        in_spec = pl.BlockSpec((step, length, rows), lambda i: (i, 0, 0))

        def write(out, pair, value):
            for n in range(2):
                half = value[:, n * rows : (n + 1) * rows]
                out[:, pair + n] = half.reshape(group, count, rows)

        def span_body(indices, w, out):
            for pair in range(0, step, 2):
                field = jnp.concatenate([w[pair], w[pair + 1]], axis=1)
                write(out, pair, product((flow_top[at], flow_low[at]), halves(field)))

        def slope_of(v, plane):
            lane = iota((length, rows), 1)
            ahead = pltpu.roll(v, rows - 1, 1)
            behind = pltpu.roll(v, 1, 1)
            low = pltpu.roll(before_ref[...], lax.rem(rows - plane, rows), 1)
            high = pltpu.roll(after_ref[...], rows - 1 - plane, 1)
            ahead = jnp.where(lane == rows - 1, high, ahead)
            behind = jnp.where(lane == 0, low, behind)
            return (ahead - behind) * gap_ref[here_y, 0:1, :]

        def flow_body(indices, u, v, out):
            first = indices.index[0] * step
            for pair in range(0, step, 2):
                field = jnp.concatenate([u[pair], u[pair + 1]], axis=1)
                value = product((slope_top[at], slope_low[at]), halves(field))
                field = jnp.concatenate(
                    [slope_of(v[pair + n], first + pair + n) for n in range(2)], axis=1
                )
                value = value + product((flow_top[at], flow_low[at]), halves(field))
                write(out, pair, value)

        if kind == 0:
            at_planes = pl.ds(start, size)
            pltpu.emit_pipeline(
                span_body, grid=(size // step,), in_specs=[in_spec], out_specs=[out_spec],
                _explicit_indices=True,
            )(velocity.at[2, at_planes], staged.at[part, 0, :, at_planes])
        else:
            pltpu.emit_pipeline(
                flow_body, grid=(planes // step,), in_specs=[in_spec] * 2, out_specs=[out_spec],
                _explicit_indices=True,
            )(velocity.at[0], velocity.at[1], staged.at[part, 1])

    def edge_body(indices, v):
        lane = iota((length, rows), 1)
        for n in range(step):
            plane = indices.index[0] * step + n
            here = lane == plane
            edges[0] = jnp.where(here, pltpu.roll(v[n], plane, 1), edges[0])
            edges[1] = jnp.where(here, pltpu.roll(v[n], lax.rem(plane + 1, rows), 1), edges[1])

    def edge_copy(side):
        far = lax.rem(here_y + (size_y - 1, 1)[side], size_y)
        return pltpu.make_async_remote_copy(
            edges.at[side],
            (after_ref, before_ref)[side],
            send_edge.at[side],
            recv_edge.at[side],
            device_id=(here_x, here_z, far),
            device_id_type=MESH,
        )

    def flow_copy(part, kind, shift, start=0, size=planes):
        far_x, far_z, far = target(shift)
        return pltpu.make_async_remote_copy(
            staged.at[part, kind, far, pl.ds(start, size)],
            landed.at[part, kind, own, pl.ds(start, size)],
            send_flow.at[part, kind, shift],
            recv_flow.at[part, kind, shift],
            device_id=(far_x, far_z, here_y),
            device_id_type=MESH,
        )

    def y_copy(part, shift):
        far = lax.rem(here_y + shift, size_y)
        return pltpu.make_async_remote_copy(
            outgoing.at[far],
            columns.at[part, :, pl.ds(pl.multiple_of(here_y * rows, rows), rows), :],
            send_y.at[part, shift],
            recv_y.at[part, shift],
            device_id=(here_x, here_z, far),
            device_id_type=MESH,
        )

    def home_copy(part, shift):
        far = lax.rem(here_y + shift, size_y)
        return pltpu.make_async_remote_copy(
            columns.at[part, :, pl.ds(pl.multiple_of(far * rows, rows), rows), :],
            returned.at[part, here_y],
            send_home.at[part, shift],
            recv_home.at[part, shift],
            device_id=(here_x, here_z, far),
            device_id_type=MESH,
        )

    def back_copy(part, shift):
        far_x, far_z, far = target(shift)
        return pltpu.make_async_remote_copy(
            back_staged.at[part, :, pl.ds(pl.multiple_of(far * planes, planes), planes), :],
            result.at[part, own],
            send_back.at[part, shift],
            recv_back.at[part, shift],
            device_id=(far_x, far_z, here_y),
            device_id_type=MESH,
        )

    first = group * count // 16
    each(0, first, flow_tables)

    def start(part, kind):
        each(1, group, lambda shift: flow_copy(part, kind, shift).start())

    def forward(part, kind):
        emit(part, kind)
        start(part, kind)

    early = min(planes, 16)
    for plane in range(0, planes, early):
        emit(0, 0, plane, early)
        each(1, group, lambda shift: flow_copy(0, 0, shift, plane, early).start())
    edges[...] = jnp.zeros_like(edges)
    pltpu.emit_pipeline(
        edge_body,
        grid=(planes // step,),
        in_specs=[pl.BlockSpec((step, length, rows), lambda i: (i, 0, 0))],
        _explicit_indices=True,
    )(velocity.at[1])
    for side in range(2):
        edge_copy(side).start()
    each(first, length // 16, flow_tables)
    for side in range(2):
        edge_copy(side).wait()
    before_ref[...] = jnp.where(here_y == 0, 0.0, before_ref[...])
    after_ref[...] = jnp.where(here_y == size_y - 1, 0.0, after_ref[...])
    forward(0, 1)

    def forward_both(part):
        forward(part, 0)
        forward(part, 1)

    ahead = min(2, parts)
    each(1, ahead, forward_both)
    each(0, span // 16, span_tables)
    each(0, length // 16, last_tables)

    def middle(part, follow):
        if follow:
            emit(part + ahead, 0)
            emit(part + ahead, 1)

        def load(kind, shift):
            owner = origin(shift)
            at = pl.ds(pl.multiple_of(owner * planes * count, planes * count), planes * count)
            return pltpu.make_async_copy(
                landed.at[part, kind, owner].reshape(planes * count, rows),
                loaded.at[kind, at],
                load_sem.at[kind, shift],
            )

        def load_own(kind):
            at = pl.ds(pl.multiple_of(own * planes * count, planes * count), planes * count)
            return pltpu.make_async_copy(
                staged.at[part, kind, own].reshape(planes * count, rows),
                loaded.at[kind, at],
                load_sem.at[kind, 0],
            )

        for kind in range(2):
            load_own(kind).start()

        def fetch(shift):
            for kind in range(2):
                flow_copy(part, kind, shift).wait_recv()
                load(kind, shift).start()

        each(1, group, fetch)
        if follow:
            start(part + ahead, 0)
            start(part + ahead, 1)
        for kind in range(2):
            load_own(kind).wait()

        def fetched(shift):
            for kind in range(2):
                load(kind, shift).wait()

        each(1, group, fetched)

        def transform(pair):
            value = None
            for kind, table in ((0, (curl_top, curl_low)), (1, (span_top, span_low))):
                field = jnp.concatenate(
                    [loaded[kind, pl.ds(pair * 2 + n, span, stride=count), :] for n in range(2)],
                    axis=1,
                )
                term = product((table[0][...], table[1][...]), halves(field))
                value = term if value is None else value + term
            for n in range(2):
                turned = value[:, n * rows : (n + 1) * rows].T
                for far in range(size_y):
                    outgoing[far, pair * 2 + n] = turned[:, far * share : (far + 1) * share]

        each(0, count // 2, transform)
        keep = pltpu.make_async_copy(
            outgoing.at[here_y],
            columns.at[part, :, pl.ds(pl.multiple_of(here_y * rows, rows), rows), :],
            local_sem.at[0],
        )
        keep.start()
        each(1, size_y, lambda shift: y_copy(part, shift).start())
        keep.wait()
        each(1, size_y, lambda shift: y_copy(part, shift).wait())
        mode = own * mode_count + part * count + iota((count, share), 0)
        span_mode = here_y * share + iota((count, share), 1)
        sigma = square_entry(mode, length, 1.0) + square_entry(span_mode, span, span_step)
        solve(
            columns.at[part].reshape(count * total, share), ratio, sides_ref, sigma, count, total
        )
        keep = pltpu.make_async_copy(
            columns.at[part, :, pl.ds(pl.multiple_of(here_y * rows, rows), rows), :],
            modes_in.at[here_y],
            local_sem.at[0],
        )
        keep.start()
        each(1, size_y, lambda shift: home_copy(part, shift).start())

        def come(shift):
            home_copy(part, shift).wait()
            far = lax.rem(here_y + size_y - shift, size_y)
            copy = pltpu.make_async_copy(
                returned.at[part, far], modes_in.at[far], load_sem.at[0, shift]
            )
            copy.start()
            copy.wait()

        each(1, size_y, come)
        keep.wait()

        def restore(pair):
            field = jnp.concatenate(
                [
                    jnp.concatenate([modes_in[k, pair * 2 + n] for k in range(size_y)], axis=1)
                    for n in range(2)
                ],
                axis=0,
            )
            value = product((inverse_top[...], inverse_low[...]), halves(field), True)
            for n in range(2):
                planes_out[pair * 2 + n] = value[:, n * rows : (n + 1) * rows]

        each(0, count // 2, restore)
        stage = pltpu.make_async_copy(planes_out, back_staged.at[part], local_sem.at[0])
        keep = pltpu.make_async_copy(
            planes_out.at[:, pl.ds(pl.multiple_of(own * planes, planes), planes), :],
            result.at[part, own],
            local_sem.at[1],
        )
        stage.start()
        keep.start()
        stage.wait()
        each(1, group, lambda shift: back_copy(part, shift).start())
        keep.wait()

    each(0, parts - ahead, lambda part: middle(part, True))
    each(parts - ahead, parts, lambda part: middle(part, False))
    depth = group * count
    tail[...] = jnp.concatenate(
        [table[:, length - depth :] for table in (last_top, last_top, last_low)], axis=1
    )
    copy = pltpu.make_async_copy(tail, tail_table, local_sem.at[0])
    copy.start()
    copy.wait()

    def arrive(part):
        each(1, group, lambda shift: back_copy(part, shift).wait_recv())

    each(0, parts - 1, arrive)
    if parts > 1:
        depth = (parts - 1) * group * count

        def sum_body(indices, r, out):
            gather(r, (last_top[:, :depth], last_low[:, :depth]), None, out)

        pltpu.emit_pipeline(
            sum_body,
            grid=(planes // 8,),
            in_specs=[pl.BlockSpec((depth, 8, rows), lambda i: (0, i, 0))],
            out_specs=[pl.BlockSpec((8, length, rows), lambda i: (i, 0, 0))],
            _explicit_indices=True,
        )(result.at[pl.ds(0, parts - 1)].reshape(depth, planes, rows), summed)
    arrive(parts - 1)

    def drain(part):
        def one(shift):
            back_copy(part, shift).wait_send()
            for kind in range(2):
                flow_copy(part, kind, shift).wait_send()

        each(1, group, one)

    each(0, parts, drain)


def gather(r, tables, base, out):
    depth, step, rows = r.shape
    flat = r.reshape(depth * step, rows)
    for pair in range(0, step, 2):
        field = jnp.concatenate(
            [flat[pl.ds(pair + n, depth, stride=step), :] for n in range(2)], axis=1
        )
        top, low = halves(field)
        if len(tables) == 1:
            stacked = jnp.concatenate([top, low, top], axis=0)
            value = jnp.dot(tables[0], stacked, preferred_element_type=f32)
        else:
            value = product(tables, (top, low))
        for n in range(2):
            half = value[:, n * rows : (n + 1) * rows]
            out[pair + n] = half if base is None else half + base[pair + n]


def finish_kernel(r, table, *refs):
    gather(r, (table[...],), refs[0] if len(refs) > 1 else None, refs[-1])


def finish(result, summed, table, parts):
    length, rows = table.shape[0], result.shape[-1]
    planes = result.shape[-2]
    depth = length // parts
    plane_spec = pl.BlockSpec((8, length, rows), lambda i: (i, 0, 0))
    bases = [summed] if parts > 1 else []
    cells = planes * length * rows
    return pl.pallas_call(
        finish_kernel,
        grid=(planes // 8,),
        out_shape=jax.ShapeDtypeStruct((planes, length, rows), f32),
        in_specs=[
            pl.BlockSpec((depth, 8, rows), lambda i: (parts - 1, i, 0)),
            pl.BlockSpec(table.shape, lambda i: (0, 0)),
        ]
        + [plane_spec] * len(bases),
        out_specs=plane_spec,
        compiler_params=pltpu.CompilerParams(vmem_limit_bytes=40 << 20),
        cost_estimate=pl.CostEstimate(
            flops=6 * cells * depth, bytes_accessed=8 * cells, transcendentals=0
        ),
    )(result.reshape(length, planes, rows), table, *bases)


def local(velocity, spacing):
    planes, length, rows = velocity.shape[1:]
    size_x, size_z, size_y = (lax.axis_size(a) for a in ("gx", "gz", "gy"))
    group = size_x * size_z
    span = planes * group
    mode_count = length // group
    parts = max(mode_count // 8, 1)
    count = mode_count // parts
    share = span // size_y
    total = rows * size_y
    step = 4
    full_width = spacing[:-1] + spacing[1:]
    sides = jnp.stack([2.0 / (full_width * spacing[:-1]), 2.0 / (full_width * spacing[1:])])
    gap = jnp.broadcast_to((1.0 / full_width).reshape(size_y, 1, rows), (size_y, 8, rows))
    vmem = pl.BlockSpec(memory_space=pltpu.VMEM)
    smem = pl.BlockSpec(memory_space=pltpu.SMEM)
    hbm = pl.BlockSpec(memory_space=pltpu.HBM)
    dma = pltpu.SemaphoreType.DMA
    outs = pl.pallas_call(
        functools.partial(
            kernel, (size_x, size_z, size_y, planes, length, rows, parts, count), step
        ),
        out_shape=[
            jax.ShapeDtypeStruct((parts, group, count, planes, rows), f32),
            jax.ShapeDtypeStruct((planes, length, rows) if parts > 1 else (8, rows), f32),
            jax.ShapeDtypeStruct((length, 3 * group * count), bf16),
            jax.ShapeDtypeStruct((parts, 2, group, planes, count, rows), f32),
            jax.ShapeDtypeStruct((parts, 2, group, planes, count, rows), f32),
            jax.ShapeDtypeStruct((parts, size_y, count, rows, share), f32),
            jax.ShapeDtypeStruct((parts, count, span, rows), f32),
        ],
        in_specs=[smem, vmem, hbm],
        out_specs=[hbm] * 7,
        scratch_shapes=[pltpu.VMEM((length, length), bf16)] * 4
        + [pltpu.VMEM((span, span), bf16)] * 6
        + [pltpu.VMEM((length, length), bf16)] * 2
        + [
            pltpu.VMEM((length, 3 * group * count), bf16),
            pltpu.VMEM((2, length, rows), f32),
            pltpu.VMEM((length, rows), f32),
            pltpu.VMEM((length, rows), f32),
            pltpu.VMEM((2, span * count, rows), f32),
            pltpu.VMEM((parts, count, total, share), f32),
            pltpu.VMEM((total, count, share), f32),
            pltpu.VMEM((size_y, count, rows, share), f32),
            pltpu.VMEM((size_y, count, rows, share), f32),
            pltpu.VMEM((count, span, rows), f32),
            dma((2,)),
            dma((2,)),
            dma((parts, 2, group)),
            dma((parts, 2, group)),
            dma((parts, size_y)),
            dma((parts, size_y)),
            dma((parts, size_y)),
            dma((parts, size_y)),
            dma((parts, group)),
            dma((parts, group)),
            dma((2, max(group, size_y))),
            dma((2,)),
        ],
        compiler_params=pltpu.CompilerParams(
            has_side_effects=True, vmem_limit_bytes=67043328
        ),
    )(sides, gap, velocity)
    return finish(*outs[:3], parts)


def solution(mesh):
    return jax.shard_map(
        local,
        mesh=mesh,
        in_specs=(P(None, ("gx", "gz"), None, "gy"), P()),
        out_specs=P(("gx", "gz"), None, "gy"),
        check_vma=False,
    )
```

```python
import functools
import math

import jax
import jax.numpy as jnp
from jax import lax
from jax.experimental import pallas as pl
from jax.experimental.pallas import tpu as pltpu
from jax.sharding import PartitionSpec as P

span_step = 0.5
f32 = jnp.float32
bf16 = jnp.bfloat16
MESH = pl.DeviceIdType.MESH


def split_by(value, size):
    if size & (size - 1):
        return lax.div(value, size), lax.rem(value, size)
    return lax.shift_right_logical(value, size.bit_length() - 1), jnp.bitwise_and(value, size - 1)


def wave_of(mode, length):
    return jnp.where(mode == 1, length // 2, lax.shift_right_logical(mode, 1))


def wave_cosine(phase, length):
    if length & (length - 1):
        phase = lax.rem(phase, length)
    else:
        phase = jnp.bitwise_and(phase, length - 1)
    phase = jnp.where(phase >= length // 2, phase - length, phase)
    return jnp.cos(2.0 * math.pi / length * phase.astype(f32))


def is_sine(mode):
    return jnp.logical_and(jnp.bitwise_and(mode, 1) == 1, mode >= 3)


def forward_entry(mode, point, length):
    phase = point * wave_of(mode, length)
    return wave_cosine(phase + jnp.where(is_sine(mode), length // 4, 0), length)


def derive_entry(mode, point, length, step_size):
    wave = wave_of(mode, length)
    phase = point * wave + jnp.where(is_sine(mode), 0, 3 * length // 4)
    kappa = 2.0 * math.pi / (length * step_size) * wave.astype(f32)
    return wave_cosine(phase, length) * jnp.where(mode >= 2, kappa, 0.0)


def inverse_entry(mode, point, length):
    weight = jnp.where(mode >= 2, 2.0, 1.0) / length
    return forward_entry(mode, point, length) * weight


def square_entry(mode, length, step_size):
    kappa = 2.0 * math.pi / (length * step_size) * wave_of(mode, length).astype(f32)
    return kappa * kappa


def halves(value):
    top = value.astype(bf16)
    return top, (value - top.astype(f32)).astype(bf16)


def product(left, right, turned=False):
    dims = (((1,), (1 if turned else 0,)), ((), ()))

    def one(a, b):
        return lax.dot_general(a, b, dims, preferred_element_type=f32)

    return one(left[0], right[0]) + (one(left[0], right[1]) + one(left[1], right[0]))


def solve(side_ref, ratio_ref, sides_ref, sigma, count, total):
    half = total // 2
    zero = jnp.zeros_like(sigma)

    def rows(row):
        return pl.ds(row, count, stride=total)

    def eliminate(step, carry):
        ratio, value, ratio_up, value_up = carry
        low, high_row = step, total - 1 - step
        lower, upper = sides_ref[0, low], sides_ref[1, low]
        inverse = 1.0 / (-(lower + upper) - sigma - lower * ratio)
        ratio = upper * inverse
        value = (side_ref[rows(low), :] - lower * value) * inverse
        ratio_ref[low] = ratio
        side_ref[rows(low), :] = value
        lower, upper = sides_ref[0, high_row], sides_ref[1, high_row]
        inverse = 1.0 / (-(lower + upper) - sigma - upper * ratio_up)
        ratio_up = lower * inverse
        value_up = (side_ref[rows(high_row), :] - upper * value_up) * inverse
        ratio_ref[high_row] = ratio_up
        side_ref[rows(high_row), :] = value_up
        return ratio, value, ratio_up, value_up

    ratio, value, ratio_up, value_up = lax.fori_loop(
        0, half, eliminate, (zero, zero, zero, zero), unroll=4
    )
    down = (value - ratio * value_up) / (1.0 - ratio * ratio_up)
    up = value_up - ratio_up * down
    side_ref[rows(half - 1), :] = down
    side_ref[rows(half), :] = up

    def substitute(step, carry):
        down, up = carry
        low, high_row = half - 2 - step, half + 1 + step
        down = side_ref[rows(low), :] - ratio_ref[low] * down
        up = side_ref[rows(high_row), :] - ratio_ref[high_row] * up
        side_ref[rows(low), :] = down
        side_ref[rows(high_row), :] = up
        return down, up

    lax.fori_loop(0, half - 1, substitute, (down, up))


def kernel(
    sizes, step, sides_ref, gap_ref, velocity, result, summed, tail_table, staged,
    landed, returned, back_staged, flow_top, flow_low, slope_top, slope_low, span_top,
    span_low, curl_top, curl_low, inverse_top, inverse_low, last_top, last_low, tail, edges, before_ref,
    after_ref, loaded, columns, ratio, outgoing, modes_in, planes_out, send_edge, recv_edge,
    send_flow, recv_flow, send_y, recv_y, send_home, recv_home, send_back, recv_back, load_sem,
    local_sem,
):
    size_x, size_z, size_y, planes, length, rows, parts, count = sizes
    group = size_x * size_z
    span = planes * group
    mode_count = parts * count
    share = span // size_y
    total = rows * size_y
    here_x, here_z, here_y = (lax.axis_index(a) for a in ("gx", "gz", "gy"))
    own = here_x * size_z + here_z

    def target(shift):
        far_x = lax.rem(here_x + shift // size_z, size_x)
        far_z = lax.rem(here_z + lax.rem(shift, size_z), size_z)
        return far_x, far_z, far_x * size_z + far_z

    def origin(shift):
        far_x = lax.rem(here_x + size_x - shift // size_z, size_x)
        far_z = lax.rem(here_z + size_z - lax.rem(shift, size_z), size_z)
        return far_x * size_z + far_z

    def each(first, last, act):
        def turn(index, carry):
            act(index)
            return carry

        lax.fori_loop(first, last, turn, 0)

    def put(top_ref, low_ref, at, value):
        top, low = halves(value)
        top_ref[at] = top
        low_ref[at] = low

    def iota(shape, axis):
        return lax.broadcasted_iota(jnp.int32, shape, axis)

    def mode_at(slot):
        part, slot = split_by(slot, group * count)
        owner, slot = split_by(slot, count)
        return owner * mode_count + part * count + slot

    def flow_tables(index):
        at = pl.ds(pl.multiple_of(index * 16, 16), 16)
        mode = mode_at(index * 16 + iota((16, length), 0))
        point = iota((16, length), 1)
        put(flow_top, flow_low, at, forward_entry(mode, point, length))
        put(slope_top, slope_low, at, derive_entry(mode, point, length, 1.0))

    def last_tables(index):
        at = pl.ds(pl.multiple_of(index * 16, 16), 16)
        point = index * 16 + iota((16, length), 0)
        mode = mode_at(iota((16, length), 1))
        put(last_top, last_low, at, inverse_entry(mode, point, length))

    def span_tables(index):
        at = pl.ds(pl.multiple_of(index * 16, 16), 16)
        line = index * 16 + iota((16, span), 0)
        across = iota((16, span), 1)
        put(span_top, span_low, at, forward_entry(line, across, span))
        put(curl_top, curl_low, at, derive_entry(line, across, span, span_step))
        put(inverse_top, inverse_low, at, inverse_entry(across, line, span))

    def emit(part, kind):
        block = group * count
        at = pl.ds(pl.multiple_of(part * block, block), block)
        out_spec = pl.BlockSpec((group, step, count, rows), lambda i: (0, i, 0, 0))
        in_spec = pl.BlockSpec((step, length, rows), lambda i: (i, 0, 0))

        def write(out, pair, value):
            for n in range(2):
                half = value[:, n * rows : (n + 1) * rows]
                out[:, pair + n] = half.reshape(group, count, rows)

        def span_body(indices, w, out):
            for pair in range(0, step, 2):
                field = jnp.concatenate([w[pair], w[pair + 1]], axis=1)
                write(out, pair, product((flow_top[at], flow_low[at]), halves(field)))

        def slope_of(v, plane):
            lane = iota((length, rows), 1)
            ahead = pltpu.roll(v, rows - 1, 1)
            behind = pltpu.roll(v, 1, 1)
            low = pltpu.roll(before_ref[...], lax.rem(rows - plane, rows), 1)
            high = pltpu.roll(after_ref[...], rows - 1 - plane, 1)
            ahead = jnp.where(lane == rows - 1, high, ahead)
            behind = jnp.where(lane == 0, low, behind)
            return (ahead - behind) * gap_ref[here_y, 0:1, :]

        def flow_body(indices, u, v, out):
            first = indices.index[0] * step
            for pair in range(0, step, 2):
                field = jnp.concatenate([u[pair], u[pair + 1]], axis=1)
                value = product((slope_top[at], slope_low[at]), halves(field))
                field = jnp.concatenate(
                    [slope_of(v[pair + n], first + pair + n) for n in range(2)], axis=1
                )
                value = value + product((flow_top[at], flow_low[at]), halves(field))
                write(out, pair, value)

        if kind == 0:
            pltpu.emit_pipeline(
                span_body, grid=(planes // step,), in_specs=[in_spec], out_specs=[out_spec],
                _explicit_indices=True,
            )(velocity.at[2], staged.at[part, 0])
        else:
            pltpu.emit_pipeline(
                flow_body, grid=(planes // step,), in_specs=[in_spec] * 2, out_specs=[out_spec],
                _explicit_indices=True,
            )(velocity.at[0], velocity.at[1], staged.at[part, 1])

    def edge_body(indices, v):
        lane = iota((length, rows), 1)
        for n in range(step):
            plane = indices.index[0] * step + n
            here = lane == plane
            edges[0] = jnp.where(here, pltpu.roll(v[n], plane, 1), edges[0])
            edges[1] = jnp.where(here, pltpu.roll(v[n], lax.rem(plane + 1, rows), 1), edges[1])

    def edge_copy(side):
        far = lax.rem(here_y + (size_y - 1, 1)[side], size_y)
        return pltpu.make_async_remote_copy(
            edges.at[side],
            (after_ref, before_ref)[side],
            send_edge.at[side],
            recv_edge.at[side],
            device_id=(here_x, here_z, far),
            device_id_type=MESH,
        )

    def flow_copy(part, kind, shift):
        far_x, far_z, far = target(shift)
        return pltpu.make_async_remote_copy(
            staged.at[part, kind, far],
            landed.at[part, kind, own],
            send_flow.at[part, kind, shift],
            recv_flow.at[part, kind, shift],
            device_id=(far_x, far_z, here_y),
            device_id_type=MESH,
        )

    def y_copy(part, shift):
        far = lax.rem(here_y + shift, size_y)
        return pltpu.make_async_remote_copy(
            outgoing.at[far],
            columns.at[part, :, pl.ds(pl.multiple_of(here_y * rows, rows), rows), :],
            send_y.at[part, shift],
            recv_y.at[part, shift],
            device_id=(here_x, here_z, far),
            device_id_type=MESH,
        )

    def home_copy(part, shift):
        far = lax.rem(here_y + shift, size_y)
        return pltpu.make_async_remote_copy(
            columns.at[part, :, pl.ds(pl.multiple_of(far * rows, rows), rows), :],
            returned.at[part, here_y],
            send_home.at[part, shift],
            recv_home.at[part, shift],
            device_id=(here_x, here_z, far),
            device_id_type=MESH,
        )

    def back_copy(part, shift):
        far_x, far_z, far = target(shift)
        return pltpu.make_async_remote_copy(
            back_staged.at[part, :, pl.ds(pl.multiple_of(far * planes, planes), planes), :],
            result.at[part, own],
            send_back.at[part, shift],
            recv_back.at[part, shift],
            device_id=(far_x, far_z, here_y),
            device_id_type=MESH,
        )

    first = group * count // 16
    each(0, first, flow_tables)

    def forward(part, kind):
        emit(part, kind)
        each(1, group, lambda shift: flow_copy(part, kind, shift).start())

    forward(0, 0)
    edges[...] = jnp.zeros_like(edges)
    pltpu.emit_pipeline(
        edge_body,
        grid=(planes // step,),
        in_specs=[pl.BlockSpec((step, length, rows), lambda i: (i, 0, 0))],
        _explicit_indices=True,
    )(velocity.at[1])
    for side in range(2):
        edge_copy(side).start()
    for side in range(2):
        edge_copy(side).wait()
    before_ref[...] = jnp.where(here_y == 0, 0.0, before_ref[...])
    after_ref[...] = jnp.where(here_y == size_y - 1, 0.0, after_ref[...])
    forward(0, 1)
    each(first, length // 16, flow_tables)

    def forward_both(part):
        forward(part, 0)
        forward(part, 1)

    each(1, parts, forward_both)
    each(0, span // 16, span_tables)
    each(0, length // 16, last_tables)

    def middle(part):
        def load(kind, shift):
            owner = origin(shift)
            at = pl.ds(pl.multiple_of(owner * planes * count, planes * count), planes * count)
            return pltpu.make_async_copy(
                landed.at[part, kind, owner].reshape(planes * count, rows),
                loaded.at[kind, at],
                load_sem.at[kind, shift],
            )

        def load_own(kind):
            at = pl.ds(pl.multiple_of(own * planes * count, planes * count), planes * count)
            return pltpu.make_async_copy(
                staged.at[part, kind, own].reshape(planes * count, rows),
                loaded.at[kind, at],
                load_sem.at[kind, 0],
            )

        for kind in range(2):
            load_own(kind).start()

        def fetch(shift):
            for kind in range(2):
                flow_copy(part, kind, shift).wait_recv()
                load(kind, shift).start()

        each(1, group, fetch)
        for kind in range(2):
            load_own(kind).wait()

        def fetched(shift):
            for kind in range(2):
                load(kind, shift).wait()

        each(1, group, fetched)

        def transform(pair):
            value = None
            for kind, table in ((0, (curl_top, curl_low)), (1, (span_top, span_low))):
                field = jnp.concatenate(
                    [loaded[kind, pl.ds(pair * 2 + n, span, stride=count), :] for n in range(2)],
                    axis=1,
                )
                term = product((table[0][...], table[1][...]), halves(field))
                value = term if value is None else value + term
            for n in range(2):
                turned = value[:, n * rows : (n + 1) * rows].T
                for far in range(size_y):
                    outgoing[far, pair * 2 + n] = turned[:, far * share : (far + 1) * share]

        each(0, count // 2, transform)
        keep = pltpu.make_async_copy(
            outgoing.at[here_y],
            columns.at[part, :, pl.ds(pl.multiple_of(here_y * rows, rows), rows), :],
            local_sem.at[0],
        )
        keep.start()
        each(1, size_y, lambda shift: y_copy(part, shift).start())
        keep.wait()
        each(1, size_y, lambda shift: y_copy(part, shift).wait())
        mode = own * mode_count + part * count + iota((count, share), 0)
        span_mode = here_y * share + iota((count, share), 1)
        sigma = square_entry(mode, length, 1.0) + square_entry(span_mode, span, span_step)
        solve(
            columns.at[part].reshape(count * total, share), ratio, sides_ref, sigma, count, total
        )
        keep = pltpu.make_async_copy(
            columns.at[part, :, pl.ds(pl.multiple_of(here_y * rows, rows), rows), :],
            modes_in.at[here_y],
            local_sem.at[0],
        )
        keep.start()
        each(1, size_y, lambda shift: home_copy(part, shift).start())

        def come(shift):
            home_copy(part, shift).wait()
            far = lax.rem(here_y + size_y - shift, size_y)
            copy = pltpu.make_async_copy(
                returned.at[part, far], modes_in.at[far], load_sem.at[0, shift]
            )
            copy.start()
            copy.wait()

        each(1, size_y, come)
        keep.wait()

        def restore(pair):
            field = jnp.concatenate(
                [
                    jnp.concatenate([modes_in[k, pair * 2 + n] for k in range(size_y)], axis=1)
                    for n in range(2)
                ],
                axis=0,
            )
            value = product((inverse_top[...], inverse_low[...]), halves(field), True)
            for n in range(2):
                planes_out[pair * 2 + n] = value[:, n * rows : (n + 1) * rows]

        each(0, count // 2, restore)
        stage = pltpu.make_async_copy(planes_out, back_staged.at[part], local_sem.at[0])
        keep = pltpu.make_async_copy(
            planes_out.at[:, pl.ds(pl.multiple_of(own * planes, planes), planes), :],
            result.at[part, own],
            local_sem.at[1],
        )
        stage.start()
        keep.start()
        stage.wait()
        each(1, group, lambda shift: back_copy(part, shift).start())
        keep.wait()

    each(0, parts, middle)
    depth = group * count
    tail[...] = jnp.concatenate(
        [table[:, length - depth :] for table in (last_top, last_top, last_low)], axis=1
    )
    copy = pltpu.make_async_copy(tail, tail_table, local_sem.at[0])
    copy.start()
    copy.wait()

    def arrive(part):
        each(1, group, lambda shift: back_copy(part, shift).wait_recv())

    each(0, parts - 1, arrive)
    if parts > 1:
        depth = (parts - 1) * group * count

        def sum_body(indices, r, out):
            gather(r, (last_top[:, :depth], last_low[:, :depth]), None, out)

        pltpu.emit_pipeline(
            sum_body,
            grid=(planes // 8,),
            in_specs=[pl.BlockSpec((depth, 8, rows), lambda i: (0, i, 0))],
            out_specs=[pl.BlockSpec((8, length, rows), lambda i: (i, 0, 0))],
            _explicit_indices=True,
        )(result.at[pl.ds(0, parts - 1)].reshape(depth, planes, rows), summed)
    arrive(parts - 1)

    def drain(part):
        def one(shift):
            back_copy(part, shift).wait_send()
            for kind in range(2):
                flow_copy(part, kind, shift).wait_send()

        each(1, group, one)

    each(0, parts, drain)


def gather(r, tables, base, out):
    depth, step, rows = r.shape
    flat = r.reshape(depth * step, rows)
    for pair in range(0, step, 2):
        field = jnp.concatenate(
            [flat[pl.ds(pair + n, depth, stride=step), :] for n in range(2)], axis=1
        )
        top, low = halves(field)
        if len(tables) == 1:
            stacked = jnp.concatenate([top, low, top], axis=0)
            value = jnp.dot(tables[0], stacked, preferred_element_type=f32)
        else:
            value = product(tables, (top, low))
        for n in range(2):
            half = value[:, n * rows : (n + 1) * rows]
            out[pair + n] = half if base is None else half + base[pair + n]


def finish_kernel(r, table, *refs):
    gather(r, (table[...],), refs[0] if len(refs) > 1 else None, refs[-1])


def finish(result, summed, table, parts):
    length, rows = table.shape[0], result.shape[-1]
    planes = result.shape[-2]
    depth = length // parts
    plane_spec = pl.BlockSpec((8, length, rows), lambda i: (i, 0, 0))
    bases = [summed] if parts > 1 else []
    cells = planes * length * rows
    return pl.pallas_call(
        finish_kernel,
        grid=(planes // 8,),
        out_shape=jax.ShapeDtypeStruct((planes, length, rows), f32),
        in_specs=[
            pl.BlockSpec((depth, 8, rows), lambda i: (parts - 1, i, 0)),
            pl.BlockSpec(table.shape, lambda i: (0, 0)),
        ]
        + [plane_spec] * len(bases),
        out_specs=plane_spec,
        compiler_params=pltpu.CompilerParams(vmem_limit_bytes=40 << 20),
        cost_estimate=pl.CostEstimate(
            flops=6 * cells * depth, bytes_accessed=8 * cells, transcendentals=0
        ),
    )(result.reshape(length, planes, rows), table, *bases)


def local(velocity, spacing):
    planes, length, rows = velocity.shape[1:]
    size_x, size_z, size_y = (lax.axis_size(a) for a in ("gx", "gz", "gy"))
    group = size_x * size_z
    span = planes * group
    mode_count = length // group
    parts = max(mode_count // 8, 1)
    count = mode_count // parts
    share = span // size_y
    total = rows * size_y
    step = 4
    full_width = spacing[:-1] + spacing[1:]
    sides = jnp.stack([2.0 / (full_width * spacing[:-1]), 2.0 / (full_width * spacing[1:])])
    gap = jnp.broadcast_to((1.0 / full_width).reshape(size_y, 1, rows), (size_y, 8, rows))
    vmem = pl.BlockSpec(memory_space=pltpu.VMEM)
    smem = pl.BlockSpec(memory_space=pltpu.SMEM)
    hbm = pl.BlockSpec(memory_space=pltpu.HBM)
    dma = pltpu.SemaphoreType.DMA
    outs = pl.pallas_call(
        functools.partial(
            kernel, (size_x, size_z, size_y, planes, length, rows, parts, count), step
        ),
        out_shape=[
            jax.ShapeDtypeStruct((parts, group, count, planes, rows), f32),
            jax.ShapeDtypeStruct((planes, length, rows) if parts > 1 else (8, rows), f32),
            jax.ShapeDtypeStruct((length, 3 * group * count), bf16),
            jax.ShapeDtypeStruct((parts, 2, group, planes, count, rows), f32),
            jax.ShapeDtypeStruct((parts, 2, group, planes, count, rows), f32),
            jax.ShapeDtypeStruct((parts, size_y, count, rows, share), f32),
            jax.ShapeDtypeStruct((parts, count, span, rows), f32),
        ],
        in_specs=[smem, vmem, hbm],
        out_specs=[hbm] * 7,
        scratch_shapes=[pltpu.VMEM((length, length), bf16)] * 4
        + [pltpu.VMEM((span, span), bf16)] * 6
        + [pltpu.VMEM((length, length), bf16)] * 2
        + [
            pltpu.VMEM((length, 3 * group * count), bf16),
            pltpu.VMEM((2, length, rows), f32),
            pltpu.VMEM((length, rows), f32),
            pltpu.VMEM((length, rows), f32),
            pltpu.VMEM((2, span * count, rows), f32),
            pltpu.VMEM((parts, count, total, share), f32),
            pltpu.VMEM((total, count, share), f32),
            pltpu.VMEM((size_y, count, rows, share), f32),
            pltpu.VMEM((size_y, count, rows, share), f32),
            pltpu.VMEM((count, span, rows), f32),
            dma((2,)),
            dma((2,)),
            dma((parts, 2, group)),
            dma((parts, 2, group)),
            dma((parts, size_y)),
            dma((parts, size_y)),
            dma((parts, size_y)),
            dma((parts, size_y)),
            dma((parts, group)),
            dma((parts, group)),
            dma((2, max(group, size_y))),
            dma((2,)),
        ],
        compiler_params=pltpu.CompilerParams(
            has_side_effects=True, vmem_limit_bytes=67043328
        ),
    )(sides, gap, velocity)
    return finish(*outs[:3], parts)


def solution(mesh):
    return jax.shard_map(
        local,
        mesh=mesh,
        in_specs=(P(None, ("gx", "gz"), None, "gy"), P()),
        out_specs=P(("gx", "gz"), None, "gy"),
        check_vma=False,
    )
```

```python
import functools
import math

import jax
import jax.numpy as jnp
from jax import lax
from jax.experimental import pallas as pl
from jax.experimental.pallas import tpu as pltpu
from jax.sharding import PartitionSpec as P

span_step = 0.5
f32 = jnp.float32
bf16 = jnp.bfloat16
MESH = pl.DeviceIdType.MESH


def split_by(value, size):
    if size & (size - 1):
        return lax.div(value, size), lax.rem(value, size)
    return lax.shift_right_logical(value, size.bit_length() - 1), jnp.bitwise_and(value, size - 1)


def wave_of(mode, length):
    return jnp.where(mode == 1, length // 2, lax.shift_right_logical(mode, 1))


def wave_cosine(phase, length):
    if length & (length - 1):
        phase = lax.rem(phase, length)
    else:
        phase = jnp.bitwise_and(phase, length - 1)
    phase = jnp.where(phase >= length // 2, phase - length, phase)
    return jnp.cos(2.0 * math.pi / length * phase.astype(f32))


def is_sine(mode):
    return jnp.logical_and(jnp.bitwise_and(mode, 1) == 1, mode >= 3)


def forward_entry(mode, point, length):
    phase = point * wave_of(mode, length)
    return wave_cosine(phase + jnp.where(is_sine(mode), length // 4, 0), length)


def derive_entry(mode, point, length, step_size):
    wave = wave_of(mode, length)
    phase = point * wave + jnp.where(is_sine(mode), 0, 3 * length // 4)
    kappa = 2.0 * math.pi / (length * step_size) * wave.astype(f32)
    return wave_cosine(phase, length) * jnp.where(mode >= 2, kappa, 0.0)


def inverse_entry(mode, point, length):
    weight = jnp.where(mode >= 2, 2.0, 1.0) / length
    return forward_entry(mode, point, length) * weight


def square_entry(mode, length, step_size):
    kappa = 2.0 * math.pi / (length * step_size) * wave_of(mode, length).astype(f32)
    return kappa * kappa


def halves(value):
    top = value.astype(bf16)
    return top, (value - top.astype(f32)).astype(bf16)


def product(left, right, turned=False):
    dims = (((1,), (1 if turned else 0,)), ((), ()))

    def one(a, b):
        return lax.dot_general(a, b, dims, preferred_element_type=f32)

    return one(left[0], right[0]) + (one(left[0], right[1]) + one(left[1], right[0]))


def solve(side_ref, ratio_ref, sides_ref, sigma, count, total):
    half = total // 2
    zero = jnp.zeros_like(sigma)

    def rows(row):
        return pl.ds(row, count, stride=total)

    def eliminate(step, carry):
        ratio, value, ratio_up, value_up = carry
        low, high_row = step, total - 1 - step
        lower, upper = sides_ref[0, low], sides_ref[1, low]
        inverse = 1.0 / (-(lower + upper) - sigma - lower * ratio)
        ratio = upper * inverse
        value = (side_ref[rows(low), :] - lower * value) * inverse
        ratio_ref[low] = ratio
        side_ref[rows(low), :] = value
        lower, upper = sides_ref[0, high_row], sides_ref[1, high_row]
        inverse = 1.0 / (-(lower + upper) - sigma - upper * ratio_up)
        ratio_up = lower * inverse
        value_up = (side_ref[rows(high_row), :] - upper * value_up) * inverse
        ratio_ref[high_row] = ratio_up
        side_ref[rows(high_row), :] = value_up
        return ratio, value, ratio_up, value_up

    ratio, value, ratio_up, value_up = lax.fori_loop(
        0, half, eliminate, (zero, zero, zero, zero), unroll=4
    )
    down = (value - ratio * value_up) / (1.0 - ratio * ratio_up)
    up = value_up - ratio_up * down
    side_ref[rows(half - 1), :] = down
    side_ref[rows(half), :] = up

    def substitute(step, carry):
        down, up = carry
        low, high_row = half - 2 - step, half + 1 + step
        down = side_ref[rows(low), :] - ratio_ref[low] * down
        up = side_ref[rows(high_row), :] - ratio_ref[high_row] * up
        side_ref[rows(low), :] = down
        side_ref[rows(high_row), :] = up
        return down, up

    lax.fori_loop(0, half - 1, substitute, (down, up))


def kernel(
    sizes, step, sides_ref, gap_ref, velocity, result, summed, tail_table, staged,
    landed, returned, back_staged, flow_top, flow_low, slope_top, slope_low, span_top,
    span_low, curl_top, curl_low, inverse_top, inverse_low, last_top, last_low, tail, edges, before_ref,
    after_ref, loaded, columns, ratio, outgoing, modes_in, planes_out, send_edge, recv_edge,
    send_flow, recv_flow, send_y, recv_y, send_home, recv_home, send_back, recv_back, load_sem,
    local_sem,
):
    size_x, size_z, size_y, planes, length, rows, parts, count = sizes
    group = size_x * size_z
    span = planes * group
    mode_count = parts * count
    share = span // size_y
    total = rows * size_y
    here_x, here_z, here_y = (lax.axis_index(a) for a in ("gx", "gz", "gy"))
    own = here_x * size_z + here_z

    def target(shift):
        far_x = lax.rem(here_x + shift // size_z, size_x)
        far_z = lax.rem(here_z + lax.rem(shift, size_z), size_z)
        return far_x, far_z, far_x * size_z + far_z

    def origin(shift):
        far_x = lax.rem(here_x + size_x - shift // size_z, size_x)
        far_z = lax.rem(here_z + size_z - lax.rem(shift, size_z), size_z)
        return far_x * size_z + far_z

    def each(first, last, act):
        def turn(index, carry):
            act(index)
            return carry

        lax.fori_loop(first, last, turn, 0)

    def put(top_ref, low_ref, at, value):
        top, low = halves(value)
        top_ref[at] = top
        low_ref[at] = low

    def iota(shape, axis):
        return lax.broadcasted_iota(jnp.int32, shape, axis)

    def mode_at(slot):
        part, slot = split_by(slot, group * count)
        owner, slot = split_by(slot, count)
        return owner * mode_count + part * count + slot

    def flow_tables(index):
        at = pl.ds(pl.multiple_of(index * 16, 16), 16)
        mode = mode_at(index * 16 + iota((16, length), 0))
        point = iota((16, length), 1)
        put(flow_top, flow_low, at, forward_entry(mode, point, length))
        put(slope_top, slope_low, at, derive_entry(mode, point, length, 1.0))

    def last_tables(index):
        at = pl.ds(pl.multiple_of(index * 16, 16), 16)
        point = index * 16 + iota((16, length), 0)
        mode = mode_at(iota((16, length), 1))
        put(last_top, last_low, at, inverse_entry(mode, point, length))

    def span_tables(index):
        at = pl.ds(pl.multiple_of(index * 16, 16), 16)
        line = index * 16 + iota((16, span), 0)
        across = iota((16, span), 1)
        put(span_top, span_low, at, forward_entry(line, across, span))
        put(curl_top, curl_low, at, derive_entry(line, across, span, span_step))
        put(inverse_top, inverse_low, at, inverse_entry(across, line, span))

    def emit(part, kind):
        block = group * count
        at = pl.ds(pl.multiple_of(part * block, block), block)
        out_spec = pl.BlockSpec((group, step, count, rows), lambda i: (0, i, 0, 0))
        in_spec = pl.BlockSpec((step, length, rows), lambda i: (i, 0, 0))

        def write(out, pair, value):
            for n in range(2):
                half = value[:, n * rows : (n + 1) * rows]
                out[:, pair + n] = half.reshape(group, count, rows)

        def span_body(indices, w, out):
            for pair in range(0, step, 2):
                field = jnp.concatenate([w[pair], w[pair + 1]], axis=1)
                write(out, pair, product((flow_top[at], flow_low[at]), halves(field)))

        def slope_of(v, plane):
            lane = iota((length, rows), 1)
            ahead = pltpu.roll(v, rows - 1, 1)
            behind = pltpu.roll(v, 1, 1)
            low = pltpu.roll(before_ref[...], lax.rem(rows - plane, rows), 1)
            high = pltpu.roll(after_ref[...], rows - 1 - plane, 1)
            ahead = jnp.where(lane == rows - 1, high, ahead)
            behind = jnp.where(lane == 0, low, behind)
            return (ahead - behind) * gap_ref[here_y, 0:1, :]

        def flow_body(indices, u, v, out):
            first = indices.index[0] * step
            for pair in range(0, step, 2):
                field = jnp.concatenate([u[pair], u[pair + 1]], axis=1)
                value = product((slope_top[at], slope_low[at]), halves(field))
                field = jnp.concatenate(
                    [slope_of(v[pair + n], first + pair + n) for n in range(2)], axis=1
                )
                value = value + product((flow_top[at], flow_low[at]), halves(field))
                write(out, pair, value)

        if kind == 0:
            pltpu.emit_pipeline(
                span_body, grid=(planes // step,), in_specs=[in_spec], out_specs=[out_spec],
                _explicit_indices=True,
            )(velocity.at[2], staged.at[part, 0])
        else:
            pltpu.emit_pipeline(
                flow_body, grid=(planes // step,), in_specs=[in_spec] * 2, out_specs=[out_spec],
                _explicit_indices=True,
            )(velocity.at[0], velocity.at[1], staged.at[part, 1])

    def edge_body(indices, v):
        lane = iota((length, rows), 1)
        for n in range(step):
            plane = indices.index[0] * step + n
            here = lane == plane
            edges[0] = jnp.where(here, pltpu.roll(v[n], plane, 1), edges[0])
            edges[1] = jnp.where(here, pltpu.roll(v[n], lax.rem(plane + 1, rows), 1), edges[1])

    def edge_copy(side):
        far = lax.rem(here_y + (size_y - 1, 1)[side], size_y)
        return pltpu.make_async_remote_copy(
            edges.at[side],
            (after_ref, before_ref)[side],
            send_edge.at[side],
            recv_edge.at[side],
            device_id=(here_x, here_z, far),
            device_id_type=MESH,
        )

    def flow_copy(part, kind, shift):
        far_x, far_z, far = target(shift)
        return pltpu.make_async_remote_copy(
            staged.at[part, kind, far],
            landed.at[part, kind, own],
            send_flow.at[part, kind, shift],
            recv_flow.at[part, kind, shift],
            device_id=(far_x, far_z, here_y),
            device_id_type=MESH,
        )

    def y_copy(part, shift):
        far = lax.rem(here_y + shift, size_y)
        return pltpu.make_async_remote_copy(
            outgoing.at[far],
            columns.at[part, :, pl.ds(pl.multiple_of(here_y * rows, rows), rows), :],
            send_y.at[part, shift],
            recv_y.at[part, shift],
            device_id=(here_x, here_z, far),
            device_id_type=MESH,
        )

    def home_copy(part, shift):
        far = lax.rem(here_y + shift, size_y)
        return pltpu.make_async_remote_copy(
            columns.at[part, :, pl.ds(pl.multiple_of(far * rows, rows), rows), :],
            returned.at[part, here_y],
            send_home.at[part, shift],
            recv_home.at[part, shift],
            device_id=(here_x, here_z, far),
            device_id_type=MESH,
        )

    def back_copy(part, shift):
        far_x, far_z, far = target(shift)
        return pltpu.make_async_remote_copy(
            back_staged.at[part, :, pl.ds(pl.multiple_of(far * planes, planes), planes), :],
            result.at[part, own],
            send_back.at[part, shift],
            recv_back.at[part, shift],
            device_id=(far_x, far_z, here_y),
            device_id_type=MESH,
        )

    first = group * count // 16
    each(0, first, flow_tables)

    def forward(part, kind):
        emit(part, kind)
        each(1, group, lambda shift: flow_copy(part, kind, shift).start())

    forward(0, 0)
    lead = min(2, parts)
    for part in range(1, lead):
        each(part * first, (part + 1) * first, flow_tables)
        forward(part, 0)
    edges[...] = jnp.zeros_like(edges)
    pltpu.emit_pipeline(
        edge_body,
        grid=(planes // step,),
        in_specs=[pl.BlockSpec((step, length, rows), lambda i: (i, 0, 0))],
        _explicit_indices=True,
    )(velocity.at[1])
    for side in range(2):
        edge_copy(side).start()
    for side in range(2):
        edge_copy(side).wait()
    before_ref[...] = jnp.where(here_y == 0, 0.0, before_ref[...])
    after_ref[...] = jnp.where(here_y == size_y - 1, 0.0, after_ref[...])
    each(0, lead, lambda part: forward(part, 1))
    each(lead * first, length // 16, flow_tables)

    def forward_both(part):
        forward(part, 0)
        forward(part, 1)

    each(lead, parts, forward_both)
    each(0, span // 16, span_tables)
    each(0, length // 16, last_tables)

    def middle(part):
        def load(kind, shift):
            owner = origin(shift)
            at = pl.ds(pl.multiple_of(owner * planes * count, planes * count), planes * count)
            return pltpu.make_async_copy(
                landed.at[part, kind, owner].reshape(planes * count, rows),
                loaded.at[kind, at],
                load_sem.at[kind, shift],
            )

        def load_own(kind):
            at = pl.ds(pl.multiple_of(own * planes * count, planes * count), planes * count)
            return pltpu.make_async_copy(
                staged.at[part, kind, own].reshape(planes * count, rows),
                loaded.at[kind, at],
                load_sem.at[kind, 0],
            )

        for kind in range(2):
            load_own(kind).start()

        def fetch(shift):
            for kind in range(2):
                flow_copy(part, kind, shift).wait_recv()
                load(kind, shift).start()

        each(1, group, fetch)
        for kind in range(2):
            load_own(kind).wait()

        def fetched(shift):
            for kind in range(2):
                load(kind, shift).wait()

        each(1, group, fetched)

        def transform(pair):
            value = None
            for kind, table in ((0, (curl_top, curl_low)), (1, (span_top, span_low))):
                field = jnp.concatenate(
                    [loaded[kind, pl.ds(pair * 2 + n, span, stride=count), :] for n in range(2)],
                    axis=1,
                )
                term = product((table[0][...], table[1][...]), halves(field))
                value = term if value is None else value + term
            for n in range(2):
                turned = value[:, n * rows : (n + 1) * rows].T
                for far in range(size_y):
                    outgoing[far, pair * 2 + n] = turned[:, far * share : (far + 1) * share]

        each(0, count // 2, transform)
        keep = pltpu.make_async_copy(
            outgoing.at[here_y],
            columns.at[part, :, pl.ds(pl.multiple_of(here_y * rows, rows), rows), :],
            local_sem.at[0],
        )
        keep.start()
        each(1, size_y, lambda shift: y_copy(part, shift).start())
        keep.wait()
        each(1, size_y, lambda shift: y_copy(part, shift).wait())
        mode = own * mode_count + part * count + iota((count, share), 0)
        span_mode = here_y * share + iota((count, share), 1)
        sigma = square_entry(mode, length, 1.0) + square_entry(span_mode, span, span_step)
        solve(
            columns.at[part].reshape(count * total, share), ratio, sides_ref, sigma, count, total
        )
        keep = pltpu.make_async_copy(
            columns.at[part, :, pl.ds(pl.multiple_of(here_y * rows, rows), rows), :],
            modes_in.at[here_y],
            local_sem.at[0],
        )
        keep.start()
        each(1, size_y, lambda shift: home_copy(part, shift).start())

        def come(shift):
            home_copy(part, shift).wait()
            far = lax.rem(here_y + size_y - shift, size_y)
            copy = pltpu.make_async_copy(
                returned.at[part, far], modes_in.at[far], load_sem.at[0, shift]
            )
            copy.start()
            copy.wait()

        each(1, size_y, come)
        keep.wait()

        def restore(pair):
            field = jnp.concatenate(
                [
                    jnp.concatenate([modes_in[k, pair * 2 + n] for k in range(size_y)], axis=1)
                    for n in range(2)
                ],
                axis=0,
            )
            value = product((inverse_top[...], inverse_low[...]), halves(field), True)
            for n in range(2):
                planes_out[pair * 2 + n] = value[:, n * rows : (n + 1) * rows]

        each(0, count // 2, restore)
        stage = pltpu.make_async_copy(planes_out, back_staged.at[part], local_sem.at[0])
        keep = pltpu.make_async_copy(
            planes_out.at[:, pl.ds(pl.multiple_of(own * planes, planes), planes), :],
            result.at[part, own],
            local_sem.at[1],
        )
        stage.start()
        keep.start()
        stage.wait()
        each(1, group, lambda shift: back_copy(part, shift).start())
        keep.wait()

    each(0, parts, middle)
    depth = group * count
    tail[...] = jnp.concatenate(
        [table[:, length - depth :] for table in (last_top, last_top, last_low)], axis=1
    )
    copy = pltpu.make_async_copy(tail, tail_table, local_sem.at[0])
    copy.start()
    copy.wait()

    def arrive(part):
        each(1, group, lambda shift: back_copy(part, shift).wait_recv())

    each(0, parts - 1, arrive)
    if parts > 1:
        depth = (parts - 1) * group * count

        def sum_body(indices, r, out):
            gather(r, (last_top[:, :depth], last_low[:, :depth]), None, out)

        pltpu.emit_pipeline(
            sum_body,
            grid=(planes // 8,),
            in_specs=[pl.BlockSpec((depth, 8, rows), lambda i: (0, i, 0))],
            out_specs=[pl.BlockSpec((8, length, rows), lambda i: (i, 0, 0))],
            _explicit_indices=True,
        )(result.at[pl.ds(0, parts - 1)].reshape(depth, planes, rows), summed)
    arrive(parts - 1)

    def drain(part):
        def one(shift):
            back_copy(part, shift).wait_send()
            for kind in range(2):
                flow_copy(part, kind, shift).wait_send()

        each(1, group, one)

    each(0, parts, drain)


def gather(r, tables, base, out):
    depth, step, rows = r.shape
    flat = r.reshape(depth * step, rows)
    for pair in range(0, step, 2):
        field = jnp.concatenate(
            [flat[pl.ds(pair + n, depth, stride=step), :] for n in range(2)], axis=1
        )
        top, low = halves(field)
        if len(tables) == 1:
            stacked = jnp.concatenate([top, low, top], axis=0)
            value = jnp.dot(tables[0], stacked, preferred_element_type=f32)
        else:
            value = product(tables, (top, low))
        for n in range(2):
            half = value[:, n * rows : (n + 1) * rows]
            out[pair + n] = half if base is None else half + base[pair + n]


def finish_kernel(r, table, *refs):
    gather(r, (table[...],), refs[0] if len(refs) > 1 else None, refs[-1])


def finish(result, summed, table, parts):
    length, rows = table.shape[0], result.shape[-1]
    planes = result.shape[-2]
    depth = length // parts
    plane_spec = pl.BlockSpec((8, length, rows), lambda i: (i, 0, 0))
    bases = [summed] if parts > 1 else []
    cells = planes * length * rows
    return pl.pallas_call(
        finish_kernel,
        grid=(planes // 8,),
        out_shape=jax.ShapeDtypeStruct((planes, length, rows), f32),
        in_specs=[
            pl.BlockSpec((depth, 8, rows), lambda i: (parts - 1, i, 0)),
            pl.BlockSpec(table.shape, lambda i: (0, 0)),
        ]
        + [plane_spec] * len(bases),
        out_specs=plane_spec,
        compiler_params=pltpu.CompilerParams(vmem_limit_bytes=40 << 20),
        cost_estimate=pl.CostEstimate(
            flops=6 * cells * depth, bytes_accessed=8 * cells, transcendentals=0
        ),
    )(result.reshape(length, planes, rows), table, *bases)


def local(velocity, spacing):
    planes, length, rows = velocity.shape[1:]
    size_x, size_z, size_y = (lax.axis_size(a) for a in ("gx", "gz", "gy"))
    group = size_x * size_z
    span = planes * group
    mode_count = length // group
    parts = max(mode_count // 8, 1)
    count = mode_count // parts
    share = span // size_y
    total = rows * size_y
    step = 4
    full_width = spacing[:-1] + spacing[1:]
    sides = jnp.stack([2.0 / (full_width * spacing[:-1]), 2.0 / (full_width * spacing[1:])])
    gap = jnp.broadcast_to((1.0 / full_width).reshape(size_y, 1, rows), (size_y, 8, rows))
    vmem = pl.BlockSpec(memory_space=pltpu.VMEM)
    smem = pl.BlockSpec(memory_space=pltpu.SMEM)
    hbm = pl.BlockSpec(memory_space=pltpu.HBM)
    dma = pltpu.SemaphoreType.DMA
    outs = pl.pallas_call(
        functools.partial(
            kernel, (size_x, size_z, size_y, planes, length, rows, parts, count), step
        ),
        out_shape=[
            jax.ShapeDtypeStruct((parts, group, count, planes, rows), f32),
            jax.ShapeDtypeStruct((planes, length, rows) if parts > 1 else (8, rows), f32),
            jax.ShapeDtypeStruct((length, 3 * group * count), bf16),
            jax.ShapeDtypeStruct((parts, 2, group, planes, count, rows), f32),
            jax.ShapeDtypeStruct((parts, 2, group, planes, count, rows), f32),
            jax.ShapeDtypeStruct((parts, size_y, count, rows, share), f32),
            jax.ShapeDtypeStruct((parts, count, span, rows), f32),
        ],
        in_specs=[smem, vmem, hbm],
        out_specs=[hbm] * 7,
        scratch_shapes=[pltpu.VMEM((length, length), bf16)] * 4
        + [pltpu.VMEM((span, span), bf16)] * 6
        + [pltpu.VMEM((length, length), bf16)] * 2
        + [
            pltpu.VMEM((length, 3 * group * count), bf16),
            pltpu.VMEM((2, length, rows), f32),
            pltpu.VMEM((length, rows), f32),
            pltpu.VMEM((length, rows), f32),
            pltpu.VMEM((2, span * count, rows), f32),
            pltpu.VMEM((parts, count, total, share), f32),
            pltpu.VMEM((total, count, share), f32),
            pltpu.VMEM((size_y, count, rows, share), f32),
            pltpu.VMEM((size_y, count, rows, share), f32),
            pltpu.VMEM((count, span, rows), f32),
            dma((2,)),
            dma((2,)),
            dma((parts, 2, group)),
            dma((parts, 2, group)),
            dma((parts, size_y)),
            dma((parts, size_y)),
            dma((parts, size_y)),
            dma((parts, size_y)),
            dma((parts, group)),
            dma((parts, group)),
            dma((2, max(group, size_y))),
            dma((2,)),
        ],
        compiler_params=pltpu.CompilerParams(
            has_side_effects=True, vmem_limit_bytes=67043328
        ),
    )(sides, gap, velocity)
    return finish(*outs[:3], parts)


def solution(mesh):
    return jax.shard_map(
        local,
        mesh=mesh,
        in_specs=(P(None, ("gx", "gz"), None, "gy"), P()),
        out_specs=P(("gx", "gz"), None, "gy"),
        check_vma=False,
    )
```
